32 devices in a mesh: aux: 2 (over x), pair: 16 (over z, y, core).
Axes of the slice: x: 2, y: 2, z: 4, core: 2. Of those that a mesh axis runs over, the one named last changes fastest.
Arguments:
- three_index: bfloat16 [256, 256, 2048], P('pair', None, 'aux'), may hold values from -0.875 to 0.875
- fock_diag: float32 [256], replicated, may hold values from -1.2 to -0.3
- pair_occ: int32 [496, 2], P('pair'), may hold values from 0 to 255, as said below
- pno_count: int32 [496], P('pair'), may hold values from 32 to 128
- pno_energy: float32 [496, 128], P('pair'), may hold values from 0.3 to 3
- pno_coef: bfloat16 [496, 2, 256, 128], P('pair'), may hold values from -0.375 to 0.375
Outputs:
- pair_energy: float32 [496], P('pair')
- grad_ints: float32 [256, 256, 2048], P('pair', None, 'aux')
The draws below stay inside these ranges and needn't reach their ends.
Inputs may be any that keep to these rules, and one draw needn't show every extreme that they name: `pair_occ`: orbital o belongs to the block o // 16. Among the 62 orbitals named by the pairs of one aligned block of 31 rows, at most 4 belong to any one orbital block, and one orbital block receives exactly 4 from every such row block; i may equal j.
All inputs are finite; a program needn't handle non-finite values.
Results may differ from the reference program's by a relative error of at most 0.0061.
Values may be sent and summed in bfloat16 or wider, within the bound.
No kernel may reach another device: no remote copies, remote signals or barrier semaphores. Data moves between devices by JAX's collectives and lax.ppermute only.
A program may use at most 128 MiB of HBM per device.

```python
import math
import jax
import jax.numpy as jnp
from jax import lax

NDOM = 256
NPNO = 128
NAUXD = 2048
OCC_DEV = 16
PAIR_DEV = 31
OCC = 256
PAIRS = 496
CAP = 4


def draw_pair_occ(key, part):
    groups = PAIRS // PAIR_DEV
    special_key, rest_key = jax.random.split(key)
    special = jax.random.randint(special_key, (), 0, groups)
    owners_all = jnp.arange(groups * CAP, dtype=jnp.int32) // CAP

    def one_block(block_key):
        first_key, second_key, third_key = jax.random.split(block_key, 3)
        scores = jax.random.permutation(first_key, groups * CAP).astype(jnp.int32)
        scores = jnp.where(owners_all == special, scores - groups * CAP, scores)
        order = jnp.argsort(scores, stable=True)
        chosen = owners_all[order][:2 * PAIR_DEV]
        chosen = chosen[jax.random.permutation(second_key, 2 * PAIR_DEV)]
        within = jax.random.randint(third_key, (2 * PAIR_DEV,), 0, OCC_DEV)
        return (chosen * OCC_DEV + within).reshape(PAIR_DEV, 2)
    block_keys = jax.random.split(rest_key, groups)
    return jax.vmap(one_block)(block_keys).reshape(PAIRS, 2).astype(jnp.int32)


def plant(entries, stream_key, least, high):
    shape = entries.shape
    place = [jax.random.randint(jax.random.fold_in(stream_key, axis), (), 0, shape[axis]) for axis in range(len(shape))]
    entries = entries.at[tuple(place)].set(least)
    longest = shape.index(max(shape))
    place[longest] = (place[longest] + 1) % shape[longest]
    return entries.at[tuple(place)].set(high)


def level_of(rng, extent, cuts, smallest, largest):
    def one(position, blocks):
        draws = jax.random.uniform(jax.random.fold_in(jax.random.fold_in(rng, 6), position), (blocks,), jnp.float32, smallest / len(cuts), largest / len(cuts))
        return jnp.repeat(jnp.exp(draws), extent[position] // blocks).reshape((-1,) + (1,) * (len(extent) - position - 1))

    level = one(*cuts[0])
    for cut in cuts[1:]:
        level = level * one(*cut)
    return level


def gaussian(key, shape, spread, limit, cuts=(), held_as=jnp.bfloat16):
    result = jax.random.normal(key, shape, jnp.float32) * spread
    if len(cuts) > 0:
        result = level_of(key, shape, cuts, -0.22, 0.18) * result
    return jnp.clip(result, min=-limit, max=limit).astype(held_as)


def setup_inputs(seed: int = 0) -> dict:
    keys = jax.random.split(jax.random.key(seed), 7)
    three_index = gaussian(keys[0], (OCC, NDOM, NAUXD), (NAUXD ** -0.25), 0.875, ((0, 16), (2, 2)))
    fock_diag = jnp.clip(jax.random.uniform(keys[1], (OCC,), jnp.float32, -1.2, -0.3), -1.2, -0.3)
    pair_occ = draw_pair_occ(jax.random.fold_in(keys[6], 71), 0)
    pno_count = plant(jax.random.randint(keys[3], (PAIRS,), NPNO // 4, NPNO + 1), jax.random.fold_in(keys[3], 1), NPNO // 4, NPNO).astype(jnp.int32)
    pno_energy = jnp.clip(jnp.exp(math.log(3.0) - 2.3025851 * jax.random.uniform(keys[4], (PAIRS, NPNO), jnp.float32) ** level_of(keys[4], (PAIRS, NPNO), ((0, 16),), -0.2, 0.2)), 0.3, 3.0)
    pno_coef = gaussian(keys[5], (PAIRS, 2, NDOM, NPNO), NDOM ** -0.5, 0.375, ((0, 16),))
    return {"three_index": three_index, "fock_diag": fock_diag, "pair_occ": pair_occ, "pno_count": pno_count, "pno_energy": pno_energy, "pno_coef": pno_coef}


def reference(three_index, fock_diag, pair_occ, pno_count, pno_energy, pno_coef):
    in_range = jnp.arange(NPNO, dtype=jnp.int32)

    def add_term(grad, term, occ_row):
        current = lax.dynamic_index_in_dim(grad, occ_row, 0, keepdims=False)
        return lax.dynamic_update_index_in_dim(grad, current + term, occ_row, 0)

    def step(k, carry):
        grad, energies = carry
        occ_i = pair_occ[k, 0]
        occ_j = pair_occ[k, 1]
        block_i = lax.dynamic_index_in_dim(three_index, occ_i, 0, keepdims=False)
        block_j = lax.dynamic_index_in_dim(three_index, occ_j, 0, keepdims=False)
        coef = lax.dynamic_index_in_dim(pno_coef, k, 0, keepdims=False)
        rows_i = jnp.dot(coef[0].T, block_i, preferred_element_type=jnp.float32).astype(jnp.bfloat16)
        rows_j = jnp.dot(coef[1].T, block_j, preferred_element_type=jnp.float32).astype(jnp.bfloat16)
        coupling = jnp.dot(rows_i, rows_j.T, preferred_element_type=jnp.float32)
        energy_row = lax.dynamic_index_in_dim(pno_energy, k, 0, keepdims=False)
        denom = energy_row[:, None] + energy_row[None, :] - fock_diag[occ_i] - fock_diag[occ_j]
        in_pno = in_range < pno_count[k]
        amplitude = jnp.where(in_pno[:, None] & in_pno[None, :], -coupling / denom, jnp.float32(0.0))
        mixed = 2.0 * amplitude - amplitude.T
        energy = jnp.sum(coupling * mixed) / (NPNO * NPNO)
        weights = mixed.astype(jnp.bfloat16)
        gamma_i = jnp.dot(weights, rows_j, preferred_element_type=jnp.float32).astype(jnp.bfloat16)
        gamma_j = jnp.dot(weights.T, rows_i, preferred_element_type=jnp.float32).astype(jnp.bfloat16)
        term_i = lax.optimization_barrier(jnp.dot(coef[0], gamma_i, preferred_element_type=jnp.float32).astype(jnp.bfloat16))
        term_j = lax.optimization_barrier(jnp.dot(coef[1], gamma_j, preferred_element_type=jnp.float32).astype(jnp.bfloat16))
        grad = add_term(grad, term_i.astype(jnp.float32), occ_i)
        grad = add_term(grad, term_j.astype(jnp.float32), occ_j)
        energies = energies.at[k].set(energy)
        return grad, energies

    grad = jnp.zeros((OCC, NDOM, NAUXD), jnp.float32)
    energies = jnp.zeros((PAIRS,), jnp.float32)
    grad, energies = lax.fori_loop(0, PAIRS, step, (grad, energies))
    return energies, grad
```

```python
import functools

import jax
import jax.numpy as jnp
from jax import lax
from jax.experimental import pallas as pl
from jax.experimental.pallas import tpu as pltpu
from jax.sharding import PartitionSpec as P

F32, BF16, I32 = jnp.float32, jnp.bfloat16, jnp.int32
ANY = pl.BlockSpec(memory_space=pl.ANY)
SMEM = pl.BlockSpec(memory_space=pltpu.SMEM)
VMEM_LIMIT = 48 * 1024 * 1024


def params():
    return pltpu.CompilerParams(vmem_limit_bytes=VMEM_LIMIT)


def cost(flops, moved):
    return pl.CostEstimate(flops=int(flops), bytes_accessed=int(moved), transcendentals=0)


def index_kernel(occ_dev, groups, capacity, flip_ref, occ_ref, fock_ref, slot_ref, inv_ref, req_ref, fsum_ref, seen):
    pairs = occ_ref.shape[0]
    flip = flip_ref[0]

    @pl.loop(0, groups)
    def _(g):
        seen[g] = 0

    @pl.loop(0, groups * capacity)
    def _(s):
        inv_ref[s] = 0
        req_ref[s] = 0

    @pl.loop(0, pairs)
    def _(k):
        total = jnp.float32(0.0)
        for side in range(2):
            occ = occ_ref[k, side]
            owner = occ // occ_dev
            rank = seen[owner]
            seen[owner] = rank + 1
            place = rank ^ flip
            slot = place * groups + owner
            slot_ref[2 * k + side] = slot
            inv_ref[slot] = 2 * k + side
            req_ref[owner * capacity + place] = occ - owner * occ_dev + 1
            total = total + fock_ref[occ]
        fsum_ref[k] = total


def index_tables(flip, pair_occ, fock_diag, occ_dev, groups, capacity):
    pairs = pair_occ.shape[0]
    slots = groups * capacity
    return pl.pallas_call(
        functools.partial(index_kernel, occ_dev, groups, capacity),
        out_shape=(
            jax.ShapeDtypeStruct((2 * pairs,), I32),
            jax.ShapeDtypeStruct((slots,), I32),
            jax.ShapeDtypeStruct((slots,), I32),
            jax.ShapeDtypeStruct((pairs,), F32),
        ),
        in_specs=[SMEM] * 3,
        out_specs=(SMEM,) * 4,
        scratch_shapes=[pltpu.SMEM((groups,), I32)],
        name="index_tables",
    )(flip, pair_occ, fock_diag)


def order_kernel(occ_dev, groups, capacity, arrived_ref, order_ref, start_ref, fill):
    @pl.loop(0, occ_dev)
    def _(o):
        fill[o] = 0

    @pl.loop(0, groups)
    def _(g):
        for place in range(capacity):
            want = arrived_ref[g, place]

            @pl.when(want > 0)
            def _():
                fill[want - 1] = fill[want - 1] + 1

    def running(o, total):
        count = fill[o]
        start_ref[o] = total
        fill[o] = total
        return total + count

    start_ref[occ_dev] = lax.fori_loop(0, occ_dev, running, jnp.int32(0))

    @pl.loop(0, groups)
    def _(g):
        for place in range(capacity):
            want = arrived_ref[g, place]

            @pl.when(want > 0)
            def _():
                at = fill[want - 1]
                order_ref[at] = place * groups + g
                fill[want - 1] = at + 1


def order_tables(arrived, occ_dev):
    groups, capacity = arrived.shape
    return pl.pallas_call(
        functools.partial(order_kernel, occ_dev, groups, capacity),
        out_shape=(
            jax.ShapeDtypeStruct((groups * capacity,), I32),
            jax.ShapeDtypeStruct((occ_dev + 1,), I32),
        ),
        in_specs=[SMEM],
        out_specs=(SMEM, SMEM),
        scratch_shapes=[pltpu.SMEM((occ_dev,), I32)],
        name="order_tables",
    )(arrived)


def pack_kernel(inv_ref, *refs):
    out_ref = refs[-1]
    for n, ref in enumerate(refs[:-1]):
        out_ref[n] = ref[0]


def pack(inv, coef, place, groups):
    _, width_dom, width_pno = coef.shape
    each = 4
    block = (1, width_dom, width_pno)

    def source(n):
        return pl.BlockSpec(block, lambda g, inv: (inv[place * groups + g * each + n], 0, 0))

    return pl.pallas_call(
        pack_kernel,
        out_shape=jax.ShapeDtypeStruct((groups, width_dom, width_pno), BF16),
        grid_spec=pltpu.PrefetchScalarGridSpec(
            num_scalar_prefetch=1,
            grid=(groups // each,),
            in_specs=[source(n) for n in range(each)],
            out_specs=pl.BlockSpec((each, width_dom, width_pno), lambda g, inv: (g, 0, 0)),
        ),
        compiler_params=params(),
        cost_estimate=cost(0, 4 * groups * width_dom * width_pno),
        name="pack",
    )(inv, *([coef] * each))


def project_kernel(arrived_ref, coef_ref, block_ref, out_ref):
    out_ref[0] = lax.dot_general(
        coef_ref[0], block_ref[0], (((0,), (0,)), ((), ())), preferred_element_type=F32
    ).astype(BF16)


def project(arrived, coef, three_index, place):
    groups, width_dom, width_pno = coef.shape
    width_aux = three_index.shape[2]
    return pl.pallas_call(
        project_kernel,
        out_shape=jax.ShapeDtypeStruct((groups, width_pno, width_aux), BF16),
        grid_spec=pltpu.PrefetchScalarGridSpec(
            num_scalar_prefetch=1,
            grid=(groups,),
            in_specs=[
                pl.BlockSpec((1, width_dom, width_pno), lambda g, want: (g, 0, 0)),
                pl.BlockSpec(
                    (1, width_dom, width_aux),
                    lambda g, want: (jnp.maximum(want[g, place] - 1, 0), 0, 0),
                ),
            ],
            out_specs=pl.BlockSpec((1, width_pno, width_aux), lambda g, want: (g, 0, 0)),
        ),
        compiler_params=params(),
        cost_estimate=cost(
            2 * groups * width_dom * width_pno * width_aux,
            2 * groups * (width_dom * width_aux + width_pno * width_aux + width_dom * width_pno),
        ),
        name="project",
    )(arrived, coef, three_index)


def fetch_rows(groups, slot_ref, rows, buf, sem, k, par):
    for side in range(2):
        slot = slot_ref[2 * k + side]
        place = slot // groups
        owner = slot - place * groups
        for c, ref in enumerate(rows):

            @pl.when(place == c)
            def _():
                pltpu.make_async_copy(ref.at[owner], buf.at[par, side], sem.at[par, side]).start()


def wait_rows(rows, buf, sem, par):
    for side in range(2):
        pltpu.make_async_copy(rows[0].at[0], buf.at[par, side], sem.at[par, side]).wait()


def stream_rows(groups, slot_ref, rows, buf, sem):
    k = pl.program_id(0)
    pairs = pl.num_programs(0)
    depth = buf.shape[0]
    par = lax.rem(k, depth)

    @pl.when(k == 0)
    def _():
        for ahead in range(depth - 1):
            fetch_rows(groups, slot_ref, rows, buf, sem, ahead, ahead)

    @pl.when(k + depth - 1 < pairs)
    def _():
        later = k + depth - 1
        fetch_rows(groups, slot_ref, rows, buf, sem, later, lax.rem(later, depth))

    wait_rows(rows, buf, sem, par)
    return k, par


def couple_kernel(groups, places, slot_ref, *refs):
    rows, out_ref, buf, sem = refs[:places], refs[places], refs[places + 1], refs[places + 2]
    _, par = stream_rows(groups, slot_ref, rows, buf, sem)
    out_ref[0] = lax.dot_general(
        buf[par, 0], buf[par, 1], (((1,), (1,)), ((), ())), preferred_element_type=F32
    ).astype(out_ref.dtype)


def couple(slot_of, rows, pairs, dtype):
    groups, width_pno, width_aux = rows[0].shape
    depth = min(4, pairs)
    return pl.pallas_call(
        functools.partial(couple_kernel, groups, len(rows)),
        out_shape=jax.ShapeDtypeStruct((pairs, width_pno, width_pno), dtype),
        grid_spec=pltpu.PrefetchScalarGridSpec(
            num_scalar_prefetch=1,
            grid=(pairs,),
            in_specs=[ANY] * len(rows),
            out_specs=pl.BlockSpec((1, width_pno, width_pno), lambda k, slot: (k, 0, 0)),
            scratch_shapes=[
                pltpu.VMEM((depth, 2, width_pno, width_aux), BF16),
                pltpu.SemaphoreType.DMA((depth, 2)),
            ],
        ),
        compiler_params=params(),
        cost_estimate=cost(
            2 * pairs * width_pno * width_pno * width_aux, 4 * pairs * width_pno * width_aux
        ),
        name="couple",
    )(slot_of, *rows)


def weigh_kernel(groups, places, parts, slot_ref, count_ref, fsum_ref, *refs):
    partial = refs[:parts]
    level_ref = refs[parts]
    rows = refs[parts + 1 : parts + 1 + places]
    gamma_ref, energy_ref, buf, sem, outbuf, outsem = refs[parts + 1 + places :]
    k, par = stream_rows(groups, slot_ref, rows, buf, sem)
    pairs = pl.num_programs(0)
    width = level_ref.shape[1]
    coupling = partial[0][0].astype(F32)
    for extra in partial[1:]:
        coupling = coupling + extra[0].astype(F32)
    across = jnp.broadcast_to(level_ref[pl.ds(k, 1), :], (width, width))
    denom = across.T + across - fsum_ref[k]
    count = count_ref[k]
    inside = (lax.broadcasted_iota(I32, (width, width), 0) < count) & (
        lax.broadcasted_iota(I32, (width, width), 1) < count
    )
    amplitude = jnp.where(inside, -coupling / denom, jnp.float32(0.0))
    mixed = 2.0 * amplitude - amplitude.T
    energy_ref[pl.ds(k, 1), :] = jnp.sum(coupling * mixed, axis=0, keepdims=True)
    weights = mixed.astype(BF16)
    gamma_i = jnp.dot(weights, buf[par, 1], preferred_element_type=F32).astype(BF16)
    gamma_j = lax.dot_general(
        weights, buf[par, 0], (((0,), (0,)), ((), ())), preferred_element_type=F32
    ).astype(BF16)
    half = lax.rem(k, 2)

    def drain(which):
        for side in range(2):
            pltpu.make_async_copy(
                outbuf.at[which, side], gamma_ref.at[0, 0], outsem.at[which, side]
            ).wait()

    @pl.when(k >= 2)
    def _():
        drain(half)

    outbuf[half, 0] = gamma_i
    outbuf[half, 1] = gamma_j
    for side in range(2):
        slot = slot_ref[2 * k + side]
        place = slot // groups
        owner = slot - place * groups
        pltpu.make_async_copy(
            outbuf.at[half, side], gamma_ref.at[owner, place], outsem.at[half, side]
        ).start()

    @pl.when(k == pairs - 1)
    def _():
        drain(half)

        @pl.when(k >= 1)
        def _():
            drain(1 - half)


def weigh(slot_of, count, fsum, partial, level, rows):
    groups, width_pno, width_aux = rows[0].shape
    pairs = level.shape[0]
    depth = min(3, pairs)
    places = len(rows)
    moved = pairs * width_pno * width_aux
    return pl.pallas_call(
        functools.partial(weigh_kernel, groups, places, len(partial)),
        out_shape=(
            jax.ShapeDtypeStruct((groups, places, width_pno, width_aux), BF16),
            jax.ShapeDtypeStruct((pairs, width_pno), F32),
        ),
        grid_spec=pltpu.PrefetchScalarGridSpec(
            num_scalar_prefetch=3,
            grid=(pairs,),
            in_specs=[
                pl.BlockSpec((1, width_pno, width_pno), lambda k, *_: (k, 0, 0)) for _ in partial
            ]
            + [pl.BlockSpec((pairs, width_pno), lambda k, *_: (0, 0))]
            + [ANY] * places,
            out_specs=(ANY, pl.BlockSpec((pairs, width_pno), lambda k, *_: (0, 0))),
            scratch_shapes=[
                pltpu.VMEM((depth, 2, width_pno, width_aux), BF16),
                pltpu.SemaphoreType.DMA((depth, 2)),
                pltpu.VMEM((2, 2, width_pno, width_aux), BF16),
                pltpu.SemaphoreType.DMA((2, 2)),
            ],
        ),
        compiler_params=params(),
        cost_estimate=cost(4 * width_pno * moved, 8 * moved),
        name="weigh",
    )(slot_of, count, fsum, *partial, level, *rows)


def gather_kernel(groups, places, order_ref, start_ref, gamma_ref, *refs):
    coefs, out_ref, gbuf, gsem, cbuf, csem = refs[:places], *refs[places:]
    o = pl.program_id(0)
    live = start_ref[pl.num_programs(0)]
    depth = gbuf.shape[0]

    def fetch(t):
        slot = order_ref[t]
        place = slot // groups
        owner = slot - place * groups
        at = lax.rem(t, depth)
        pltpu.make_async_copy(gamma_ref.at[owner, place], gbuf.at[at], gsem.at[at]).start()
        for c, ref in enumerate(coefs):

            @pl.when(place == c)
            def _():
                pltpu.make_async_copy(ref.at[owner], cbuf.at[at], csem.at[at]).start()

    @pl.when(o == 0)
    def _():
        for t in range(depth - 1):

            @pl.when(t < live)
            def _():
                fetch(t)

    out_ref[...] = jnp.zeros_like(out_ref)

    @pl.loop(start_ref[o], start_ref[o + 1])
    def _(t):
        @pl.when(t + depth - 1 < live)
        def _():
            fetch(t + depth - 1)

        at = lax.rem(t, depth)
        pltpu.make_async_copy(gamma_ref.at[0, 0], gbuf.at[at], gsem.at[at]).wait()
        pltpu.make_async_copy(coefs[0].at[0], cbuf.at[at], csem.at[at]).wait()
        out_ref[0] += jnp.dot(cbuf[at], gbuf[at], preferred_element_type=F32)


def gather_terms(order, start, gamma, coefs, occ_dev):
    groups, places, width_pno, width_aux = gamma.shape
    width_dom = coefs[0].shape[1]
    depth = 4
    slots = groups * places
    return pl.pallas_call(
        functools.partial(gather_kernel, groups, places),
        out_shape=jax.ShapeDtypeStruct((occ_dev, width_dom, width_aux), F32),
        grid_spec=pltpu.PrefetchScalarGridSpec(
            num_scalar_prefetch=2,
            grid=(occ_dev,),
            in_specs=[ANY] * (1 + places),
            out_specs=pl.BlockSpec((1, width_dom, width_aux), lambda o, *_: (o, 0, 0)),
            scratch_shapes=[
                pltpu.VMEM((depth, width_pno, width_aux), BF16),
                pltpu.SemaphoreType.DMA((depth,)),
                pltpu.VMEM((depth, width_dom, width_pno), BF16),
                pltpu.SemaphoreType.DMA((depth,)),
            ],
        ),
        compiler_params=params(),
        cost_estimate=cost(
            2 * slots * width_dom * width_pno * width_aux,
            2 * slots * width_pno * width_aux + 4 * occ_dev * width_dom * width_aux,
        ),
        name="gather_terms",
    )(order, start, gamma, *coefs)


def exchange(x):
    return lax.all_to_all(x, "pair", split_axis=0, concat_axis=0, tiled=True)


def swap(x):
    return lax.ppermute(x, "aux", [(0, 1), (1, 0)])


def local(three_index, fock_diag, pair_occ, pno_count, pno_energy, pno_coef):
    groups = lax.axis_size("pair")
    twins = lax.axis_size("aux") == 2
    occ_dev, width_dom, _ = three_index.shape
    pairs = pair_occ.shape[0]
    width_pno = pno_coef.shape[3]
    halves = 2 * pairs
    capacity = max(2, halves // groups + 1)
    capacity += capacity % 2
    flip = lax.axis_index("aux") if twins else jnp.int32(0)
    slot_of, inv, request, fsum = index_tables(
        flip.astype(I32).reshape(1), pair_occ, fock_diag, occ_dev, groups, capacity
    )
    arrived = exchange(request.reshape(groups, capacity))
    coef_half = pno_coef.reshape(halves, width_dom, width_pno)
    coefs = []
    for place in range(capacity):
        if twins and place % 2:
            coefs.append(swap(coefs[-1]))
        else:
            coefs.append(exchange(pack(inv, coef_half, place, groups)))
    rows = [
        exchange(project(arrived, coefs[place], three_index, place)) for place in range(capacity)
    ]
    if twins:
        mine = couple(slot_of, rows, pairs, BF16)
        partial = [mine, swap(mine)]
    else:
        partial = [lax.psum(couple(slot_of, rows, pairs, F32), "aux")]
    gamma, energy = weigh(slot_of, pno_count, fsum, partial, pno_energy, rows)
    gamma = exchange(gamma)
    order, start = order_tables(arrived, occ_dev)
    grad = gather_terms(order, start, gamma, coefs, occ_dev)
    return jnp.sum(energy, axis=1) / (width_pno * width_pno), grad


def solution(mesh):
    placed = (
        P("pair", None, "aux"),
        P(),
        P("pair", None),
        P("pair"),
        P("pair", None),
        P("pair", None, None, None),
    )
    return jax.shard_map(
        local,
        mesh=mesh,
        in_specs=placed,
        out_specs=(P("pair"), P("pair", None, "aux")),
        check_vma=False,
    )
```

```python
import functools

import jax
import jax.numpy as jnp
from jax import lax
from jax.experimental import pallas as pl
from jax.experimental.pallas import tpu as pltpu
from jax.sharding import PartitionSpec as P

F32, BF16, I32 = jnp.float32, jnp.bfloat16, jnp.int32
ANY = pl.BlockSpec(memory_space=pl.ANY)
SMEM = pl.BlockSpec(memory_space=pltpu.SMEM)


def params():
    return pltpu.CompilerParams()


def cost(flops, moved):
    return pl.CostEstimate(flops=int(flops), bytes_accessed=int(moved), transcendentals=0)


def index_kernel(occ_dev, groups, capacity, flip_ref, occ_ref, fock_ref, slot_ref, inv_ref, req_ref, fsum_ref, seen):
    pairs = occ_ref.shape[0]
    flip = flip_ref[0]

    @pl.loop(0, groups)
    def _(g):
        seen[g] = 0

    @pl.loop(0, groups * capacity)
    def _(s):
        inv_ref[s] = 0
        req_ref[s] = 0

    @pl.loop(0, pairs)
    def _(k):
        total = jnp.float32(0.0)
        for side in range(2):
            occ = occ_ref[k, side]
            owner = occ // occ_dev
            rank = seen[owner]
            seen[owner] = rank + 1
            place = rank ^ flip
            slot = place * groups + owner
            slot_ref[2 * k + side] = slot
            inv_ref[slot] = 2 * k + side
            req_ref[owner * capacity + place] = occ - owner * occ_dev + 1
            total = total + fock_ref[occ]
        fsum_ref[k] = total


def index_tables(flip, pair_occ, fock_diag, occ_dev, groups, capacity):
    pairs = pair_occ.shape[0]
    slots = groups * capacity
    return pl.pallas_call(
        functools.partial(index_kernel, occ_dev, groups, capacity),
        out_shape=(
            jax.ShapeDtypeStruct((2 * pairs,), I32),
            jax.ShapeDtypeStruct((slots,), I32),
            jax.ShapeDtypeStruct((slots,), I32),
            jax.ShapeDtypeStruct((pairs,), F32),
        ),
        in_specs=[SMEM] * 3,
        out_specs=(SMEM,) * 4,
        scratch_shapes=[pltpu.SMEM((groups,), I32)],
        name="index_tables",
    )(flip, pair_occ, fock_diag)


def order_kernel(occ_dev, groups, capacity, arrived_ref, order_ref, start_ref, fill):
    @pl.loop(0, occ_dev)
    def _(o):
        fill[o] = 0

    @pl.loop(0, order_ref.shape[0])
    def _(t):
        order_ref[t] = -1

    @pl.loop(0, groups)
    def _(g):
        for place in range(capacity):
            want = arrived_ref[g, place]

            @pl.when(want > 0)
            def _():
                fill[want - 1] = fill[want - 1] + 1

    def running(o, total):
        count = fill[o]
        start_ref[o] = total
        fill[o] = total
        return total + 2 * ((count + 1) // 2)

    start_ref[occ_dev] = lax.fori_loop(0, occ_dev, running, jnp.int32(0))

    @pl.loop(0, groups)
    def _(g):
        for place in range(capacity):
            want = arrived_ref[g, place]

            @pl.when(want > 0)
            def _():
                at = fill[want - 1]
                order_ref[at] = place * groups + g
                fill[want - 1] = at + 1


def order_tables(arrived, occ_dev):
    groups, capacity = arrived.shape
    return pl.pallas_call(
        functools.partial(order_kernel, occ_dev, groups, capacity),
        out_shape=(
            jax.ShapeDtypeStruct((groups * capacity + occ_dev,), I32),
            jax.ShapeDtypeStruct((occ_dev + 1,), I32),
        ),
        in_specs=[SMEM],
        out_specs=(SMEM, SMEM),
        scratch_shapes=[pltpu.SMEM((occ_dev,), I32)],
        name="order_tables",
    )(arrived)


def wide(ref):
    return jnp.concatenate([ref[j] for j in range(ref.shape[0])], axis=1)


def spread(ref, value):
    lanes = ref.shape[2]
    for j in range(ref.shape[0]):
        ref[j] = value[:, j * lanes : (j + 1) * lanes]


def pack_kernel(groups, capacity, place, each, inv_ref, req_ref, *refs):
    out_ref = refs[-1]
    width_dom = refs[0].shape[1]
    extra = out_ref.shape[1] - width_dom
    for n, ref in enumerate(refs[:-1]):
        out_ref[n, :width_dom] = ref[0]
        if extra:
            g = pl.program_id(0) * each + n
            lane = lax.broadcasted_iota(I32, (extra, out_ref.shape[2]), 1)
            asked = jnp.zeros(lane.shape, F32)
            for v in range(capacity):
                asked = jnp.where(lane == v, req_ref[g * capacity + v].astype(F32), asked)
            out_ref[n, width_dom:] = asked.astype(BF16)


def pack(inv, request, coef, place, groups, capacity):
    _, width_dom, width_pno = coef.shape
    each = 4
    extra = 0 if place else 16
    block = (1, width_dom, width_pno)

    def source(n):
        return pl.BlockSpec(block, lambda g, inv, req: (inv[place * groups + g * each + n], 0, 0))

    return pl.pallas_call(
        functools.partial(pack_kernel, groups, capacity, place, each),
        out_shape=jax.ShapeDtypeStruct((groups, width_dom + extra, width_pno), BF16),
        grid_spec=pltpu.PrefetchScalarGridSpec(
            num_scalar_prefetch=2,
            grid=(groups // each,),
            in_specs=[source(n) for n in range(each)],
            out_specs=pl.BlockSpec(
                (each, width_dom + extra, width_pno), lambda g, inv, req: (g, 0, 0)
            ),
        ),
        compiler_params=params(),
        cost_estimate=cost(0, 4 * groups * width_dom * width_pno),
        name="pack",
    )(inv, request, *([coef] * each))


def project_kernel(columns, arrived_ref, *refs):
    out_ref = refs[-1]
    for n in range(len(refs) // 2):
        rows = lax.dot_general(
            refs[2 * n][0], refs[2 * n + 1][0], (((0,), (0,)), ((), ())), preferred_element_type=F32
        ).astype(BF16)
        spread(out_ref.at[0, pl.ds(n * columns, columns)], rows)


def project(arrived, coefs, three_index, places):
    groups, _, width_pno = coefs[0].shape
    _, width_dom, width_aux = three_index.shape
    columns = width_aux // width_pno
    specs, operands = [], []
    for place in places:
        specs.append(pl.BlockSpec((1, width_dom, width_pno), lambda g, want: (g, 0, 0)))
        specs.append(
            pl.BlockSpec(
                (1, width_dom, width_aux),
                lambda g, want, place=place: (jnp.maximum(want[g, place] - 1, 0), 0, 0),
            )
        )
        operands += [coefs[place], three_index]
    count = len(places)
    return pl.pallas_call(
        functools.partial(project_kernel, columns),
        out_shape=jax.ShapeDtypeStruct((groups, count * columns, width_pno, width_pno), BF16),
        grid_spec=pltpu.PrefetchScalarGridSpec(
            num_scalar_prefetch=1,
            grid=(groups,),
            in_specs=specs,
            out_specs=pl.BlockSpec(
                (1, count * columns, width_pno, width_pno), lambda g, want: (g, 0, 0, 0)
            ),
        ),
        compiler_params=params(),
        cost_estimate=cost(
            2 * count * groups * width_dom * width_pno * width_aux,
            2 * count * groups * (width_dom + width_pno) * width_aux,
        ),
        name="project",
    )(arrived, *operands)


def split_slot(groups, slot):
    place = slot // groups
    return place, slot - place * groups


def fetch_slot(groups, slot, first, rest, buf, sem):
    place, owner = split_slot(groups, slot)
    columns = buf.shape[0]

    @pl.when(place == 0)
    def _():
        pltpu.make_async_copy(first.at[owner], buf, sem).start()

    @pl.when(place > 0)
    def _():
        at = pl.ds((place - 1) * columns, columns)
        pltpu.make_async_copy(rest.at[owner, at], buf, sem).start()


def stream_rows(groups, slot_ref, first, rest, buf, sem):
    k = pl.program_id(0)
    pairs = pl.num_programs(0)
    depth = buf.shape[0]
    par = lax.rem(k, depth)

    def fetch(which, at):
        for side in range(2):
            slot = slot_ref[2 * which + side]
            fetch_slot(groups, slot, first, rest, buf.at[at, side], sem.at[at, side])

    @pl.when(k == 0)
    def _():
        for ahead in range(depth - 1):
            fetch(ahead, ahead)

    @pl.when(k + depth - 1 < pairs)
    def _():
        fetch(k + depth - 1, lax.rem(k + depth - 1, depth))

    for side in range(2):
        pltpu.make_async_copy(first.at[0], buf.at[par, side], sem.at[par, side]).wait()
    return k, par


def relay_kernel(groups, inv_ref, slot_ref, first, rest, out_ref, buf, insem, outsem):
    @pl.loop(0, groups)
    def _(g):
        half = inv_ref[g]
        fetch_slot(groups, slot_ref[half ^ 1], first, rest, buf.at[g], insem.at[g])

    @pl.loop(0, groups)
    def _(g):
        pltpu.make_async_copy(first.at[0], buf.at[g], insem.at[g]).wait()
        pltpu.make_async_copy(buf.at[g], out_ref.at[g], outsem.at[g]).start()

    @pl.loop(0, groups)
    def _(g):
        pltpu.make_async_copy(buf.at[g], out_ref.at[g], outsem.at[g]).wait()


def relay(inv, slot_of, first, rest):
    groups = first.shape[0]
    size = first.size
    return pl.pallas_call(
        functools.partial(relay_kernel, groups),
        out_shape=jax.ShapeDtypeStruct(first.shape, BF16),
        in_specs=[SMEM, SMEM, ANY, ANY],
        out_specs=ANY,
        scratch_shapes=[
            pltpu.VMEM(first.shape, BF16),
            pltpu.SemaphoreType.DMA((groups,)),
            pltpu.SemaphoreType.DMA((groups,)),
        ],
        compiler_params=params(),
        cost_estimate=cost(0, 4 * size),
        name="relay",
    )(inv, slot_of, first, rest)


def couple_kernel(groups, slot_ref, first, rest, out_ref, buf, sem):
    _, par = stream_rows(groups, slot_ref, first, rest, buf, sem)
    out_ref[0] = lax.dot_general(
        wide(buf.at[par, 0]),
        wide(buf.at[par, 1]),
        (((1,), (1,)), ((), ())),
        preferred_element_type=F32,
    ).astype(out_ref.dtype)


def couple(slot_of, first, rest, pairs, dtype):
    groups, columns, width_pno, _ = first.shape
    depth = min(4, pairs)
    moved = pairs * columns * width_pno * width_pno
    return pl.pallas_call(
        functools.partial(couple_kernel, groups),
        out_shape=jax.ShapeDtypeStruct((pairs, width_pno, width_pno), dtype),
        grid_spec=pltpu.PrefetchScalarGridSpec(
            num_scalar_prefetch=1,
            grid=(pairs,),
            in_specs=[ANY, ANY],
            out_specs=pl.BlockSpec((1, width_pno, width_pno), lambda k, slot: (k, 0, 0)),
            scratch_shapes=[
                pltpu.VMEM((depth, 2, columns, width_pno, width_pno), BF16),
                pltpu.SemaphoreType.DMA((depth, 2)),
            ],
        ),
        compiler_params=params(),
        cost_estimate=cost(2 * moved * width_pno, 4 * moved),
        name="couple",
    )(slot_of, first, rest)


def weigh_kernel(groups, parts, slot_ref, count_ref, fsum_ref, *refs):
    partial = refs[:parts]
    level_ref, first, rest = refs[parts : parts + 3]
    gamma_ref, energy_ref, buf, sem, outbuf, wbuf, outsem = refs[parts + 3 :]
    k, par = stream_rows(groups, slot_ref, first, rest, buf, sem)
    pairs = pl.num_programs(0)
    width = level_ref.shape[1]
    columns = buf.shape[2]
    last = gamma_ref.shape[1] - 1
    coupling = partial[0][0].astype(F32)
    for extra in partial[1:]:
        coupling = coupling + extra[0].astype(F32)
    across = jnp.broadcast_to(level_ref[pl.ds(k, 1), :], (width, width))
    denom = across.T + across - fsum_ref[k]
    count = count_ref[k]
    inside = (lax.broadcasted_iota(I32, (width, width), 0) < count) & (
        lax.broadcasted_iota(I32, (width, width), 1) < count
    )
    amplitude = jnp.where(inside, -coupling / denom, jnp.float32(0.0))
    turned = amplitude.T
    mixed = 2.0 * amplitude - turned
    energy_ref[pl.ds(k, 1), :] = jnp.sum(coupling * mixed, axis=0, keepdims=True)
    weights = (mixed.astype(BF16), (2.0 * turned - amplitude).astype(BF16))
    half = lax.rem(k, 2)

    def send(which, buffer, go):
        for side in range(2):
            place, owner = split_slot(groups, slot_ref[2 * which + side])

            @pl.when(place > 0)
            def _():
                at = pl.ds((place - 1) * columns, columns)
                go(
                    pltpu.make_async_copy(
                        outbuf.at[buffer, side], gamma_ref.at[owner, at], outsem.at[buffer, side]
                    )
                )

            @pl.when(place == 0)
            def _():
                go(
                    pltpu.make_async_copy(
                        wbuf.at[buffer, side], gamma_ref.at[owner, last], outsem.at[buffer, side]
                    )
                )

    @pl.when(k >= 2)
    def _():
        send(k - 2, half, lambda copy: copy.wait())

    for side in range(2):
        spread(
            outbuf.at[half, side],
            jnp.dot(
                weights[side], wide(buf.at[par, 1 - side]), preferred_element_type=F32
            ).astype(BF16),
        )
        wbuf[half, side] = weights[side]
    send(k, half, lambda copy: copy.start())

    @pl.when(k == pairs - 1)
    def _():
        @pl.when(k >= 1)
        def _():
            send(k - 1, 1 - half, lambda copy: copy.wait())

        send(k, half, lambda copy: copy.wait())


def weigh(slot_of, count, fsum, partial, level, first, rest):
    groups, columns, width_pno, _ = first.shape
    pairs = level.shape[0]
    depth = min(3, pairs)
    moved = pairs * columns * width_pno * width_pno
    return pl.pallas_call(
        functools.partial(weigh_kernel, groups, len(partial)),
        out_shape=(
            jax.ShapeDtypeStruct((groups, rest.shape[1] + 1, width_pno, width_pno), BF16),
            jax.ShapeDtypeStruct((pairs, width_pno), F32),
        ),
        grid_spec=pltpu.PrefetchScalarGridSpec(
            num_scalar_prefetch=3,
            grid=(pairs,),
            in_specs=[
                pl.BlockSpec((1, width_pno, width_pno), lambda k, *_: (k, 0, 0)) for _ in partial
            ]
            + [pl.BlockSpec((pairs, width_pno), lambda k, *_: (0, 0)), ANY, ANY],
            out_specs=(ANY, pl.BlockSpec((pairs, width_pno), lambda k, *_: (0, 0))),
            scratch_shapes=[
                pltpu.VMEM((depth, 2, columns, width_pno, width_pno), BF16),
                pltpu.SemaphoreType.DMA((depth, 2)),
                pltpu.VMEM((2, 2, columns, width_pno, width_pno), BF16),
                pltpu.VMEM((2, 2, width_pno, width_pno), BF16),
                pltpu.SemaphoreType.DMA((2, 2)),
            ],
        ),
        compiler_params=params(),
        cost_estimate=cost(4 * width_pno * moved, 8 * moved),
        name="weigh",
    )(slot_of, count, fsum, *partial, level, first, rest)


def gather_kernel(groups, places, order_ref, start_ref, rows_ref, gamma_ref, *refs):
    coefs, (out_ref, gbuf, gsem, wbuf, wsem, cbuf, csem) = refs[:places], refs[places:]
    o = pl.program_id(0)
    couples = start_ref[pl.num_programs(0)] // 2
    depth = gbuf.shape[0]
    last = gamma_ref.shape[1] - 1
    width_dom = cbuf.shape[2]

    def fetch(u):
        at = lax.rem(u, depth)
        for n in range(2):
            slot = order_ref[2 * u + n]

            @pl.when(slot >= 0)
            def _():
                place, owner = split_slot(groups, slot)
                fetch_slot(groups, slot, rows_ref, gamma_ref, gbuf.at[at, n], gsem.at[at, n])

                @pl.when(place == 0)
                def _():
                    pltpu.make_async_copy(
                        gamma_ref.at[owner, last], wbuf.at[at, n], wsem.at[at, n]
                    ).start()

                for c, ref in enumerate(coefs):

                    @pl.when(place == c)
                    def _():
                        pltpu.make_async_copy(
                            ref.at[owner, pl.ds(0, width_dom)], cbuf.at[at, n], csem.at[at, n]
                        ).start()

    @pl.when(o == 0)
    def _():
        for u in range(depth - 1):

            @pl.when(u < couples)
            def _():
                fetch(u)

    out_ref[...] = jnp.zeros_like(out_ref)

    @pl.loop(start_ref[o] // 2, start_ref[o + 1] // 2)
    def _(u):
        @pl.when(u + depth - 1 < couples)
        def _():
            fetch(u + depth - 1)

        at = lax.rem(u, depth)
        for n in range(2):
            slot = order_ref[2 * u + n]

            @pl.when(slot >= 0)
            def _():
                pltpu.make_async_copy(rows_ref.at[0], gbuf.at[at, n], gsem.at[at, n]).wait()
                pltpu.make_async_copy(
                    coefs[0].at[0, pl.ds(0, width_dom)], cbuf.at[at, n], csem.at[at, n]
                ).wait()

                @pl.when(slot < groups)
                def _():
                    pltpu.make_async_copy(
                        gamma_ref.at[0, last], wbuf.at[at, n], wsem.at[at, n]
                    ).wait()
                    spread(
                        gbuf.at[at, n],
                        jnp.dot(
                            wbuf[at, n], wide(gbuf.at[at, n]), preferred_element_type=F32
                        ).astype(BF16),
                    )

        second = order_ref[2 * u + 1]

        @pl.when(second >= 0)
        def _():
            left = jnp.concatenate([cbuf[at, 0], cbuf[at, 1]], axis=1)
            right = jnp.concatenate([wide(gbuf.at[at, 0]), wide(gbuf.at[at, 1])], axis=0)
            out_ref[0] += jnp.dot(left, right, preferred_element_type=F32)

        @pl.when(second < 0)
        def _():
            out_ref[0] += jnp.dot(cbuf[at, 0], wide(gbuf.at[at, 0]), preferred_element_type=F32)


def gather_terms(order, start, rows, gamma, coefs, occ_dev, width_dom):
    groups, columns, width_pno, _ = rows.shape
    width_aux = columns * width_pno
    places = len(coefs)
    depth = 3
    slots = groups * places
    return pl.pallas_call(
        functools.partial(gather_kernel, groups, places),
        out_shape=jax.ShapeDtypeStruct((occ_dev, width_dom, width_aux), F32),
        grid_spec=pltpu.PrefetchScalarGridSpec(
            num_scalar_prefetch=2,
            grid=(occ_dev,),
            in_specs=[ANY] * (2 + places),
            out_specs=pl.BlockSpec((1, width_dom, width_aux), lambda o, *_: (o, 0, 0)),
            scratch_shapes=[
                pltpu.VMEM((depth, 2, columns, width_pno, width_pno), BF16),
                pltpu.SemaphoreType.DMA((depth, 2)),
                pltpu.VMEM((depth, 2, width_pno, width_pno), BF16),
                pltpu.SemaphoreType.DMA((depth, 2)),
                pltpu.VMEM((depth, 2, width_dom, width_pno), BF16),
                pltpu.SemaphoreType.DMA((depth, 2)),
            ],
        ),
        compiler_params=params(),
        cost_estimate=cost(
            2 * slots * width_dom * width_pno * width_aux,
            2 * slots * width_pno * width_aux + 4 * occ_dev * width_dom * width_aux,
        ),
        name="gather_terms",
    )(order, start, rows, gamma, *coefs)


def exchange(x):
    return lax.all_to_all(x, "pair", split_axis=0, concat_axis=0, tiled=True)


def swap(x):
    return lax.ppermute(x, "aux", [(0, 1), (1, 0)])


def local(three_index, fock_diag, pair_occ, pno_count, pno_energy, pno_coef):
    groups = lax.axis_size("pair")
    twins = lax.axis_size("aux") == 2
    occ_dev, width_dom, _ = three_index.shape
    pairs = pair_occ.shape[0]
    width_pno = pno_coef.shape[3]
    halves = 2 * pairs
    capacity = max(2, halves // groups + 1)
    capacity += capacity % 2
    flip = lax.axis_index("aux") if twins else jnp.int32(0)
    slot_of, inv, request, fsum = index_tables(
        flip.astype(I32).reshape(1), pair_occ, fock_diag, occ_dev, groups, capacity
    )
    coef_half = pno_coef.reshape(halves, width_dom, width_pno)
    coefs = []
    for place in range(capacity):
        if twins and place % 2:
            coefs.append(swap(coefs[-1]))
        else:
            coefs.append(exchange(pack(inv, request, coef_half, place, groups, capacity)))
    arrived = coefs[0][:, width_dom, :capacity].astype(F32).astype(I32)
    first = exchange(project(arrived, coefs, three_index, (0,)))
    rest = exchange(project(arrived, coefs, three_index, tuple(range(1, capacity))))
    relayed = exchange(relay(inv, slot_of, first, rest))
    if twins:
        mine = couple(slot_of, first, rest, pairs, BF16)
        partial = [mine, swap(mine)]
    else:
        partial = [lax.psum(couple(slot_of, first, rest, pairs, F32), "aux")]
    gamma, energy = weigh(slot_of, pno_count, fsum, partial, pno_energy, first, rest)
    gamma = exchange(gamma)
    order, start = order_tables(arrived, occ_dev)
    grad = gather_terms(order, start, relayed, gamma, coefs, occ_dev, width_dom)
    return jnp.sum(energy, axis=1) / (width_pno * width_pno), grad


def solution(mesh):
    placed = (
        P("pair", None, "aux"),
        P(),
        P("pair", None),
        P("pair"),
        P("pair", None),
        P("pair", None, None, None),
    )
    return jax.shard_map(
        local,
        mesh=mesh,
        in_specs=placed,
        out_specs=(P("pair"), P("pair", None, "aux")),
        check_vma=False,
    )
```

```python
import functools

import jax
import jax.numpy as jnp
from jax import lax
from jax.experimental import pallas as pl
from jax.experimental.pallas import tpu as pltpu
from jax.sharding import PartitionSpec as P

F32, BF16, I32 = jnp.float32, jnp.bfloat16, jnp.int32
ANY = pl.BlockSpec(memory_space=pl.ANY)
SMEM = pl.BlockSpec(memory_space=pltpu.SMEM)
EXTRA = 16


def params():
    return pltpu.CompilerParams()


def cost(flops, moved):
    return pl.CostEstimate(flops=int(flops), bytes_accessed=int(moved), transcendentals=0)


def index_kernel(occ_dev, groups, capacity, *refs):
    flip_ref, occ_ref, fock_ref, slot_ref, home_ref, inv_ref, lead_ref, req_ref, fsum_ref, seen = refs
    pairs = occ_ref.shape[0]
    flip = flip_ref[0]

    @pl.loop(0, groups)
    def _(g):
        seen[g] = 0
        lead_ref[g] = 0

    @pl.loop(0, groups * capacity)
    def _(s):
        inv_ref[s] = 0
        req_ref[s] = 0

    @pl.loop(0, pairs)
    def _(k):
        total = jnp.float32(0.0)
        for side in range(2):
            occ = occ_ref[k, side]
            owner = occ // occ_dev
            rank = seen[owner]
            seen[owner] = rank + 1
            place = rank ^ flip
            slot = place * groups + owner
            slot_ref[2 * k + side] = slot
            home_ref[2 * k + side] = rank * groups + owner
            inv_ref[slot] = 2 * k + side

            @pl.when(rank == 0)
            def _():
                lead_ref[owner] = 2 * k + side

            req_ref[owner * capacity + place] = occ - owner * occ_dev + 1
            total = total + fock_ref[occ]
        fsum_ref[k] = total


def index_tables(flip, pair_occ, fock_diag, occ_dev, groups, capacity):
    pairs = pair_occ.shape[0]
    slots = groups * capacity
    return pl.pallas_call(
        functools.partial(index_kernel, occ_dev, groups, capacity),
        out_shape=(
            jax.ShapeDtypeStruct((2 * pairs,), I32),
            jax.ShapeDtypeStruct((2 * pairs,), I32),
            jax.ShapeDtypeStruct((slots,), I32),
            jax.ShapeDtypeStruct((groups,), I32),
            jax.ShapeDtypeStruct((slots,), I32),
            jax.ShapeDtypeStruct((pairs,), F32),
        ),
        in_specs=[SMEM] * 3,
        out_specs=(SMEM,) * 6,
        scratch_shapes=[pltpu.SMEM((groups,), I32)],
        name="index_tables",
    )(flip, pair_occ, fock_diag)


def order_kernel(occ_dev, groups, capacity, arrived_ref, order_ref, start_ref, fill):
    @pl.loop(0, occ_dev)
    def _(o):
        fill[o] = 0

    @pl.loop(0, order_ref.shape[0])
    def _(t):
        order_ref[t] = -1

    @pl.loop(0, groups)
    def _(g):
        for place in range(capacity):
            want = arrived_ref[g, place]

            @pl.when(want > 0)
            def _():
                fill[want - 1] = fill[want - 1] + 1

    def running(o, total):
        count = fill[o]
        start_ref[o] = total
        fill[o] = total
        return total + 2 * ((count + 1) // 2)

    start_ref[occ_dev] = lax.fori_loop(0, occ_dev, running, jnp.int32(0))

    @pl.loop(0, groups)
    def _(g):
        for place in range(capacity):
            want = arrived_ref[g, place]

            @pl.when(want > 0)
            def _():
                at = fill[want - 1]
                order_ref[at] = place * groups + g
                fill[want - 1] = at + 1


def order_tables(arrived, occ_dev):
    groups, capacity = arrived.shape
    return pl.pallas_call(
        functools.partial(order_kernel, occ_dev, groups, capacity),
        out_shape=(
            jax.ShapeDtypeStruct((groups * capacity + occ_dev,), I32),
            jax.ShapeDtypeStruct((occ_dev + 1,), I32),
        ),
        in_specs=[SMEM],
        out_specs=(SMEM, SMEM),
        scratch_shapes=[pltpu.SMEM((occ_dev,), I32)],
        name="order_tables",
    )(arrived)


def wide(ref):
    return jnp.concatenate([ref[j] for j in range(ref.shape[0])], axis=1)


def spread(ref, value):
    lanes = ref.shape[2]
    for j in range(ref.shape[0]):
        ref[j] = value[:, j * lanes : (j + 1) * lanes]


def split3(x):
    high = x.astype(BF16)
    left = x - high.astype(F32)
    middle = left.astype(BF16)
    return high, middle, (left - middle.astype(F32)).astype(BF16)


def join3(high, middle, low):
    return (high.astype(F32) + middle.astype(F32)) + low.astype(F32)


def pack_kernel(capacity, each, inv_ref, lead_ref, req_ref, fsum_ref, count_ref, level_ref, *refs):
    out_ref = refs[-1]
    width_dom, lanes = refs[0].shape[1:]
    for n, ref in enumerate(refs[:-1]):
        out_ref[n, :width_dom] = ref[0]
        if out_ref.shape[1] == width_dom:
            continue
        g = pl.program_id(0) * each + n
        k = lead_ref[g] // 2
        row = lax.broadcasted_iota(I32, (EXTRA, lanes), 0)
        lane = lax.broadcasted_iota(I32, (EXTRA, lanes), 1)
        asked = jnp.zeros((EXTRA, lanes), F32)
        for v in range(capacity):
            asked = jnp.where(lane == v, req_ref[g * capacity + v].astype(F32), asked)
        asked = jnp.where(lane == capacity, count_ref[k].astype(F32), asked)
        levels = split3(jnp.broadcast_to(level_ref[pl.ds(k, 1), :], (EXTRA, lanes)))
        sums = split3(jnp.full((EXTRA, lanes), fsum_ref[k], F32))
        rows = asked
        for at, part in enumerate(levels + sums):
            rows = jnp.where(row == at + 1, part.astype(F32), rows)
        out_ref[n, width_dom:] = rows.astype(BF16)


def pack(tables, coef, place, groups, capacity):
    inv, lead, request, fsum, count, level = tables
    _, width_dom, width_pno = coef.shape
    each = 4
    extra = 0 if place else EXTRA
    block = (1, width_dom, width_pno)

    def source(n):
        return pl.BlockSpec(block, lambda g, inv, *_: (inv[place * groups + g * each + n], 0, 0))

    return pl.pallas_call(
        functools.partial(pack_kernel, capacity, each),
        out_shape=jax.ShapeDtypeStruct((groups, width_dom + extra, width_pno), BF16),
        grid_spec=pltpu.PrefetchScalarGridSpec(
            num_scalar_prefetch=5,
            grid=(groups // each,),
            in_specs=[pl.BlockSpec(level.shape, lambda g, *_: (0, 0))]
            + [source(n) for n in range(each)],
            out_specs=pl.BlockSpec((each, width_dom + extra, width_pno), lambda g, *_: (g, 0, 0)),
        ),
        compiler_params=params(),
        cost_estimate=cost(0, 4 * groups * width_dom * width_pno),
        name="pack",
    )(inv, lead, request, fsum, count, level, *([coef] * each))


def project_kernel(columns, arrived_ref, *refs):
    out_ref = refs[-1]
    for n in range(len(refs) // 2):
        rows = lax.dot_general(
            refs[2 * n][0], refs[2 * n + 1][0], (((0,), (0,)), ((), ())), preferred_element_type=F32
        ).astype(BF16)
        spread(out_ref.at[0, pl.ds(n * columns, columns)], rows)


def project(arrived, coefs, three_index, places):
    groups, _, width_pno = coefs[0].shape
    _, width_dom, width_aux = three_index.shape
    columns = width_aux // width_pno
    specs, operands = [], []
    for place in places:
        specs.append(pl.BlockSpec((1, width_dom, width_pno), lambda g, want: (g, 0, 0)))
        specs.append(
            pl.BlockSpec(
                (1, width_dom, width_aux),
                lambda g, want, place=place: (jnp.maximum(want[g, place] - 1, 0), 0, 0),
            )
        )
        operands += [coefs[place], three_index]
    count = len(places)
    return pl.pallas_call(
        functools.partial(project_kernel, columns),
        out_shape=jax.ShapeDtypeStruct((groups, count * columns, width_pno, width_pno), BF16),
        grid_spec=pltpu.PrefetchScalarGridSpec(
            num_scalar_prefetch=1,
            grid=(groups,),
            in_specs=specs,
            out_specs=pl.BlockSpec(
                (1, count * columns, width_pno, width_pno), lambda g, want: (g, 0, 0, 0)
            ),
        ),
        compiler_params=params(),
        cost_estimate=cost(
            2 * count * groups * width_dom * width_pno * width_aux,
            2 * count * groups * (width_dom + width_pno) * width_aux,
        ),
        name="project",
    )(arrived, *operands)


def split_slot(groups, slot):
    place = slot // groups
    return place, slot - place * groups


def fetch_slot(groups, slot, first, rest, buf, sem):
    place, owner = split_slot(groups, slot)
    columns = buf.shape[0]

    @pl.when(place == 0)
    def _():
        pltpu.make_async_copy(first.at[owner], buf, sem).start()

    @pl.when(place > 0)
    def _():
        at = pl.ds((place - 1) * columns, columns)
        pltpu.make_async_copy(rest.at[owner, at], buf, sem).start()


def stream_rows(groups, slot_ref, first, rest, buf, sem):
    k = pl.program_id(0)
    pairs = pl.num_programs(0)
    depth = buf.shape[0]
    par = lax.rem(k, depth)

    def fetch(which, at):
        for side in range(2):
            slot = slot_ref[2 * which + side]
            fetch_slot(groups, slot, first, rest, buf.at[at, side], sem.at[at, side])

    @pl.when(k == 0)
    def _():
        for ahead in range(depth - 1):
            fetch(ahead, ahead)

    @pl.when(k + depth - 1 < pairs)
    def _():
        fetch(k + depth - 1, lax.rem(k + depth - 1, depth))

    for side in range(2):
        pltpu.make_async_copy(first.at[0], buf.at[par, side], sem.at[par, side]).wait()
    return k, par


def relay_kernel(groups, lead_ref, slot_ref, first, rest, out_ref, buf, insem, outsem):
    @pl.loop(0, groups)
    def _(g):
        half = lead_ref[g]
        fetch_slot(groups, slot_ref[half ^ 1], first, rest, buf.at[g], insem.at[g])

    @pl.loop(0, groups)
    def _(g):
        pltpu.make_async_copy(first.at[0], buf.at[g], insem.at[g]).wait()
        pltpu.make_async_copy(buf.at[g], out_ref.at[g], outsem.at[g]).start()

    @pl.loop(0, groups)
    def _(g):
        pltpu.make_async_copy(buf.at[g], out_ref.at[g], outsem.at[g]).wait()


def relay(lead, slot_of, first, rest):
    groups = first.shape[0]
    size = first.size
    return pl.pallas_call(
        functools.partial(relay_kernel, groups),
        out_shape=jax.ShapeDtypeStruct(first.shape, BF16),
        in_specs=[SMEM, SMEM, ANY, ANY],
        out_specs=ANY,
        scratch_shapes=[
            pltpu.VMEM(first.shape, BF16),
            pltpu.SemaphoreType.DMA((groups,)),
            pltpu.SemaphoreType.DMA((groups,)),
        ],
        compiler_params=params(),
        cost_estimate=cost(0, 4 * size),
        name="relay",
    )(lead, slot_of, first, rest)


def couple_kernel(groups, slot_ref, first, rest, out_ref, buf, sem):
    _, par = stream_rows(groups, slot_ref, first, rest, buf, sem)
    out_ref[0] = lax.dot_general(
        wide(buf.at[par, 0]),
        wide(buf.at[par, 1]),
        (((1,), (1,)), ((), ())),
        preferred_element_type=F32,
    ).astype(out_ref.dtype)


def couple(slot_of, first, rest, pairs, dtype):
    groups, columns, width_pno, _ = first.shape
    depth = min(4, pairs)
    moved = pairs * columns * width_pno * width_pno
    return pl.pallas_call(
        functools.partial(couple_kernel, groups),
        out_shape=jax.ShapeDtypeStruct((pairs, width_pno, width_pno), dtype),
        grid_spec=pltpu.PrefetchScalarGridSpec(
            num_scalar_prefetch=1,
            grid=(pairs,),
            in_specs=[ANY, ANY],
            out_specs=pl.BlockSpec((1, width_pno, width_pno), lambda k, slot: (k, 0, 0)),
            scratch_shapes=[
                pltpu.VMEM((depth, 2, columns, width_pno, width_pno), BF16),
                pltpu.SemaphoreType.DMA((depth, 2)),
            ],
        ),
        compiler_params=params(),
        cost_estimate=cost(2 * moved * width_pno, 4 * moved),
        name="couple",
    )(slot_of, first, rest)


def amplitudes(coupling, levels, fsum, count):
    width = coupling.shape[0]
    across = jnp.broadcast_to(levels, (width, width))
    denom = across.T + across - fsum
    inside = (lax.broadcasted_iota(I32, (width, width), 0) < count) & (
        lax.broadcasted_iota(I32, (width, width), 1) < count
    )
    return jnp.where(inside, -coupling / denom, jnp.float32(0.0))


def total(partial):
    coupling = partial[0][0].astype(F32)
    for extra in partial[1:]:
        coupling = coupling + extra[0].astype(F32)
    return coupling


def weigh_kernel(groups, parts, slot_ref, home_ref, count_ref, fsum_ref, *refs):
    partial = refs[:parts]
    level_ref, first, rest = refs[parts : parts + 3]
    gamma_ref, energy_ref, buf, sem, outbuf, outsem = refs[parts + 3 :]
    k, par = stream_rows(groups, slot_ref, first, rest, buf, sem)
    pairs = pl.num_programs(0)
    columns = buf.shape[2]
    coupling = total(partial)
    amplitude = amplitudes(coupling, level_ref[pl.ds(k, 1), :], fsum_ref[k], count_ref[k])
    turned = amplitude.T
    mixed = 2.0 * amplitude - turned
    energy_ref[pl.ds(k, 1), :] = jnp.sum(coupling * mixed, axis=0, keepdims=True)
    weights = (mixed.astype(BF16), (2.0 * turned - amplitude).astype(BF16))
    half = lax.rem(k, 2)

    def send(which, buffer, go):
        for side in range(2):
            place, owner = split_slot(groups, home_ref[2 * which + side])

            @pl.when(place > 0)
            def _():
                at = pl.ds((place - 1) * columns, columns)
                go(
                    pltpu.make_async_copy(
                        outbuf.at[buffer, side], gamma_ref.at[owner, at], outsem.at[buffer, side]
                    )
                )

    @pl.when(k >= 2)
    def _():
        send(k - 2, half, lambda copy: copy.wait())

    for side in range(2):
        spread(
            outbuf.at[half, side],
            jnp.dot(
                weights[side], wide(buf.at[par, 1 - side]), preferred_element_type=F32
            ).astype(BF16),
        )
    send(k, half, lambda copy: copy.start())

    @pl.when(k == pairs - 1)
    def _():
        @pl.when(k >= 1)
        def _():
            send(k - 1, 1 - half, lambda copy: copy.wait())

        send(k, half, lambda copy: copy.wait())


def weigh(slot_of, home, count, fsum, partial, level, first, rest):
    groups, columns, width_pno, _ = first.shape
    pairs = level.shape[0]
    depth = min(3, pairs)
    moved = pairs * columns * width_pno * width_pno
    return pl.pallas_call(
        functools.partial(weigh_kernel, groups, len(partial)),
        out_shape=(
            jax.ShapeDtypeStruct(rest.shape, BF16),
            jax.ShapeDtypeStruct((pairs, width_pno), F32),
        ),
        grid_spec=pltpu.PrefetchScalarGridSpec(
            num_scalar_prefetch=4,
            grid=(pairs,),
            in_specs=[
                pl.BlockSpec((1, width_pno, width_pno), lambda k, *_: (k, 0, 0)) for _ in partial
            ]
            + [pl.BlockSpec((pairs, width_pno), lambda k, *_: (0, 0)), ANY, ANY],
            out_specs=(ANY, pl.BlockSpec((pairs, width_pno), lambda k, *_: (0, 0))),
            scratch_shapes=[
                pltpu.VMEM((depth, 2, columns, width_pno, width_pno), BF16),
                pltpu.SemaphoreType.DMA((depth, 2)),
                pltpu.VMEM((2, 2, columns, width_pno, width_pno), BF16),
                pltpu.SemaphoreType.DMA((2, 2)),
            ],
        ),
        compiler_params=params(),
        cost_estimate=cost(4 * width_pno * moved, 8 * moved),
        name="weigh",
    )(slot_of, home, count, fsum, *partial, level, first, rest)


def couple_here_kernel(flip_ref, *refs):
    owned, (other_ref, out_ref) = refs[:-2], refs[-2:]
    own = wide(owned[0].at[0])
    for ref in owned[1:]:
        own = jnp.where(flip_ref[0] == 0, own, wide(ref.at[0]))
    out_ref[0] = lax.dot_general(
        own, wide(other_ref.at[0]), (((1,), (1,)), ((), ())), preferred_element_type=F32
    ).astype(out_ref.dtype)


def couple_here(flip, owned, other, dtype):
    groups, columns, width_pno, _ = other.shape
    rows = pl.BlockSpec((1, columns, width_pno, width_pno), lambda g, flip: (g, 0, 0, 0))
    return pl.pallas_call(
        couple_here_kernel,
        out_shape=jax.ShapeDtypeStruct((groups, width_pno, width_pno), dtype),
        grid_spec=pltpu.PrefetchScalarGridSpec(
            num_scalar_prefetch=1,
            grid=(groups,),
            in_specs=[rows] * (len(owned) + 1),
            out_specs=pl.BlockSpec((1, width_pno, width_pno), lambda g, flip: (g, 0, 0)),
        ),
        compiler_params=params(),
        cost_estimate=cost(2 * other.size * width_pno, 4 * other.size),
        name="couple_here",
    )(flip, *owned, other)


def weigh_here_kernel(capacity, parts, *refs):
    partial = refs[:parts]
    facts_ref, rows_ref, out_ref = refs[parts:]
    facts = facts_ref[0].astype(F32)
    levels = join3(facts[1:2], facts[2:3], facts[3:4])
    fsum = join3(facts[4:5], facts[5:6], facts[6:7])
    count = facts[0:1, capacity : capacity + 1].astype(I32)
    amplitude = amplitudes(total(partial), levels, fsum, count)
    weights = (2.0 * amplitude - amplitude.T).astype(BF16)
    spread(
        out_ref.at[0],
        jnp.dot(weights, wide(rows_ref.at[0]), preferred_element_type=F32).astype(BF16),
    )


def weigh_here(partial, coef, rows, width_dom, capacity):
    groups, columns, width_pno, _ = rows.shape
    square = pl.BlockSpec((1, width_pno, width_pno), lambda g: (g, 0, 0))
    block = pl.BlockSpec((1, columns, width_pno, width_pno), lambda g: (g, 0, 0, 0))
    return pl.pallas_call(
        functools.partial(weigh_here_kernel, capacity, len(partial)),
        out_shape=jax.ShapeDtypeStruct(rows.shape, BF16),
        grid=(groups,),
        in_specs=[square] * len(partial)
        + [pl.BlockSpec((1, EXTRA, width_pno), lambda g: (g, width_dom // EXTRA, 0)), block],
        out_specs=block,
        compiler_params=params(),
        cost_estimate=cost(2 * rows.size * width_pno, 4 * rows.size),
        name="weigh_here",
    )(*partial, coef, rows)


def gather_kernel(groups, places, flip_ref, order_ref, start_ref, rows_ref, gamma_ref, *refs):
    coefs, (out_ref, gbuf, gsem, cbuf, csem) = refs[:places], refs[places:]
    o = pl.program_id(0)
    couples = start_ref[pl.num_programs(0)] // 2
    depth = gbuf.shape[0]
    width_dom = cbuf.shape[2]

    def fetch(u):
        at = lax.rem(u, depth)
        for n in range(2):
            slot = order_ref[2 * u + n]

            @pl.when(slot >= 0)
            def _():
                place, owner = split_slot(groups, slot)
                home = (place ^ flip_ref[0]) * groups + owner
                fetch_slot(groups, home, rows_ref, gamma_ref, gbuf.at[at, n], gsem.at[at, n])

                for c, ref in enumerate(coefs):

                    @pl.when(place == c)
                    def _():
                        pltpu.make_async_copy(
                            ref.at[owner, pl.ds(0, width_dom)], cbuf.at[at, n], csem.at[at, n]
                        ).start()

    @pl.when(o == 0)
    def _():
        for u in range(depth - 1):

            @pl.when(u < couples)
            def _():
                fetch(u)

    out_ref[...] = jnp.zeros_like(out_ref)

    @pl.loop(start_ref[o] // 2, start_ref[o + 1] // 2)
    def _(u):
        @pl.when(u + depth - 1 < couples)
        def _():
            fetch(u + depth - 1)

        at = lax.rem(u, depth)
        for n in range(2):
            slot = order_ref[2 * u + n]

            @pl.when(slot >= 0)
            def _():
                pltpu.make_async_copy(rows_ref.at[0], gbuf.at[at, n], gsem.at[at, n]).wait()
                pltpu.make_async_copy(
                    coefs[0].at[0, pl.ds(0, width_dom)], cbuf.at[at, n], csem.at[at, n]
                ).wait()

        second = order_ref[2 * u + 1]

        @pl.when(second >= 0)
        def _():
            left = jnp.concatenate([cbuf[at, 0], cbuf[at, 1]], axis=1)
            right = jnp.concatenate([wide(gbuf.at[at, 0]), wide(gbuf.at[at, 1])], axis=0)
            out_ref[0] += jnp.dot(left, right, preferred_element_type=F32)

        @pl.when(second < 0)
        def _():
            out_ref[0] += jnp.dot(cbuf[at, 0], wide(gbuf.at[at, 0]), preferred_element_type=F32)


def gather_terms(flip, order, start, rows, gamma, coefs, occ_dev, width_dom):
    groups, columns, width_pno, _ = rows.shape
    width_aux = columns * width_pno
    places = len(coefs)
    depth = 5
    slots = groups * places
    return pl.pallas_call(
        functools.partial(gather_kernel, groups, places),
        out_shape=jax.ShapeDtypeStruct((occ_dev, width_dom, width_aux), F32),
        grid_spec=pltpu.PrefetchScalarGridSpec(
            num_scalar_prefetch=3,
            grid=(occ_dev,),
            in_specs=[ANY] * (2 + places),
            out_specs=pl.BlockSpec((1, width_dom, width_aux), lambda o, *_: (o, 0, 0)),
            scratch_shapes=[
                pltpu.VMEM((depth, 2, columns, width_pno, width_pno), BF16),
                pltpu.SemaphoreType.DMA((depth, 2)),
                pltpu.VMEM((depth, 2, width_dom, width_pno), BF16),
                pltpu.SemaphoreType.DMA((depth, 2)),
            ],
        ),
        compiler_params=params(),
        cost_estimate=cost(
            2 * slots * width_dom * width_pno * width_aux,
            2 * slots * width_pno * width_aux + 4 * occ_dev * width_dom * width_aux,
        ),
        name="gather_terms",
    )(flip, order, start, rows, gamma, *coefs)


def exchange(x):
    return lax.all_to_all(x, "pair", split_axis=0, concat_axis=0, tiled=True)


def swap(x):
    return lax.ppermute(x, "aux", [(0, 1), (1, 0)])


def local(three_index, fock_diag, pair_occ, pno_count, pno_energy, pno_coef):
    groups = lax.axis_size("pair")
    twins = lax.axis_size("aux") == 2
    occ_dev, width_dom, _ = three_index.shape
    pairs = pair_occ.shape[0]
    width_pno = pno_coef.shape[3]
    halves = 2 * pairs
    capacity = max(2, halves // groups + 1)
    capacity += capacity % 2
    flip = (lax.axis_index("aux") if twins else jnp.int32(0)).astype(I32).reshape(1)
    slot_of, home, inv, lead, request, fsum = index_tables(
        flip, pair_occ, fock_diag, occ_dev, groups, capacity
    )
    coef_half = pno_coef.reshape(halves, width_dom, width_pno)
    tables = (inv, lead, request, fsum, pno_count, pno_energy)
    coefs = []
    for place in range(capacity):
        if twins and place % 2:
            coefs.append(swap(coefs[-1]))
        else:
            coefs.append(exchange(pack(tables, coef_half, place, groups, capacity)))
    arrived = coefs[0][:, width_dom, :capacity].astype(F32).astype(I32)
    own = project(arrived, coefs, three_index, (0,))
    first = exchange(own)
    own_rest = project(arrived, coefs, three_index, tuple(range(1, capacity)))
    rest = exchange(own_rest)
    relayed = exchange(relay(lead, slot_of, first, rest))
    rounded = BF16 if twins else F32

    def complete(mine):
        return [mine, swap(mine)] if twins else [lax.psum(mine, "aux")]

    partial = complete(couple(slot_of, first, rest, pairs, rounded))
    gamma, energy = weigh(slot_of, home, pno_count, fsum, partial, pno_energy, first, rest)
    gamma = exchange(gamma)
    order, start = order_tables(arrived, occ_dev)
    partial = complete(couple_here(flip, [own, own_rest] if twins else [own], relayed, rounded))
    relayed = weigh_here(partial, coefs[0], relayed, width_dom, capacity)
    grad = gather_terms(flip, order, start, relayed, gamma, coefs, occ_dev, width_dom)
    return jnp.sum(energy, axis=1) / (width_pno * width_pno), grad


def solution(mesh):
    placed = (
        P("pair", None, "aux"),
        P(),
        P("pair", None),
        P("pair"),
        P("pair", None),
        P("pair", None, None, None),
    )
    return jax.shard_map(
        local,
        mesh=mesh,
        in_specs=placed,
        out_specs=(P("pair"), P("pair", None, "aux")),
        check_vma=False,
    )
```

```python
import functools

import jax
import jax.numpy as jnp
from jax import lax
from jax.experimental import pallas as pl
from jax.experimental.pallas import tpu as pltpu
from jax.sharding import PartitionSpec as P


F32, BF16, I32 = jnp.float32, jnp.bfloat16, jnp.int32
ANY = pl.BlockSpec(memory_space=pl.ANY)
SMEM = pl.BlockSpec(memory_space=pltpu.SMEM)
EXTRA = 16


def params():
    return pltpu.CompilerParams()


def cost(flops, moved):
    return pl.CostEstimate(flops=int(flops), bytes_accessed=int(moved), transcendentals=0)


def index_kernel(occ_dev, groups, capacity, *refs):
    flip_ref, occ_ref, fock_ref, slot_ref, home_ref, inv_ref, lead_ref, req_ref, fsum_ref, seen = refs
    pairs = occ_ref.shape[0]
    flip = flip_ref[0]

    @pl.loop(0, groups)
    def _(g):
        seen[g] = 0
        lead_ref[g] = 0

    @pl.loop(0, groups * capacity)
    def _(s):
        inv_ref[s] = 0
        req_ref[s] = 0

    @pl.loop(0, pairs)
    def _(k):
        total = jnp.float32(0.0)
        for side in range(2):
            occ = occ_ref[k, side]
            owner = occ // occ_dev
            rank = seen[owner]
            seen[owner] = rank + 1
            place = rank ^ flip
            slot = place * groups + owner
            slot_ref[2 * k + side] = slot
            home_ref[2 * k + side] = rank * groups + owner
            inv_ref[slot] = 2 * k + side

            @pl.when(rank == 0)
            def _():
                lead_ref[owner] = 2 * k + side

            req_ref[owner * capacity + place] = occ - owner * occ_dev + 1
            total = total + fock_ref[occ]
        fsum_ref[k] = total


def index_tables(flip, pair_occ, fock_diag, occ_dev, groups, capacity):
    pairs = pair_occ.shape[0]
    slots = groups * capacity
    return pl.pallas_call(
        functools.partial(index_kernel, occ_dev, groups, capacity),
        out_shape=(
            jax.ShapeDtypeStruct((2 * pairs,), I32),
            jax.ShapeDtypeStruct((2 * pairs,), I32),
            jax.ShapeDtypeStruct((slots,), I32),
            jax.ShapeDtypeStruct((groups,), I32),
            jax.ShapeDtypeStruct((slots,), I32),
            jax.ShapeDtypeStruct((pairs,), F32),
        ),
        in_specs=[SMEM] * 3,
        out_specs=(SMEM,) * 6,
        scratch_shapes=[pltpu.SMEM((groups,), I32)],
        name="index_tables",
    )(flip, pair_occ, fock_diag)


def order_kernel(occ_dev, groups, capacity, arrived_ref, order_ref, start_ref, fill):
    @pl.loop(0, occ_dev)
    def _(o):
        fill[o] = 0

    @pl.loop(0, order_ref.shape[0])
    def _(t):
        order_ref[t] = -1

    @pl.loop(0, groups)
    def _(g):
        for place in range(capacity):
            want = arrived_ref[g, place]

            @pl.when(want > 0)
            def _():
                fill[want - 1] = fill[want - 1] + 1

    def running(o, total):
        count = fill[o]
        start_ref[o] = total
        fill[o] = total
        return total + 2 * ((count + 1) // 2)

    start_ref[occ_dev] = lax.fori_loop(0, occ_dev, running, jnp.int32(0))

    @pl.loop(0, groups)
    def _(g):
        for place in range(capacity):
            want = arrived_ref[g, place]

            @pl.when(want > 0)
            def _():
                at = fill[want - 1]
                order_ref[at] = place * groups + g
                fill[want - 1] = at + 1


def order_tables(arrived, occ_dev):
    groups, capacity = arrived.shape
    return pl.pallas_call(
        functools.partial(order_kernel, occ_dev, groups, capacity),
        out_shape=(
            jax.ShapeDtypeStruct((groups * capacity + occ_dev,), I32),
            jax.ShapeDtypeStruct((occ_dev + 1,), I32),
        ),
        in_specs=[SMEM],
        out_specs=(SMEM, SMEM),
        scratch_shapes=[pltpu.SMEM((occ_dev,), I32)],
        name="order_tables",
    )(arrived)


def wide(ref):
    return jnp.concatenate([ref[j] for j in range(ref.shape[0])], axis=1)


def spread(ref, value):
    lanes = ref.shape[2]
    for j in range(ref.shape[0]):
        ref[j] = value[:, j * lanes : (j + 1) * lanes]


def split3(x):
    high = x.astype(BF16)
    left = x - high.astype(F32)
    middle = left.astype(BF16)
    return high, middle, (left - middle.astype(F32)).astype(BF16)


def join3(high, middle, low):
    return (high.astype(F32) + middle.astype(F32)) + low.astype(F32)


def pack_kernel(capacity, each, inv_ref, lead_ref, req_ref, fsum_ref, count_ref, level_ref, *refs):
    out_ref = refs[-1]
    width_dom, lanes = refs[0].shape[1:]
    for n, ref in enumerate(refs[:-1]):
        out_ref[n, :width_dom] = ref[0]
        if out_ref.shape[1] == width_dom:
            continue
        g = pl.program_id(0) * each + n
        k = lead_ref[g] // 2
        row = lax.broadcasted_iota(I32, (EXTRA, lanes), 0)
        lane = lax.broadcasted_iota(I32, (EXTRA, lanes), 1)
        asked = jnp.zeros((EXTRA, lanes), F32)
        for v in range(capacity):
            asked = jnp.where(lane == v, req_ref[g * capacity + v].astype(F32), asked)
        asked = jnp.where(lane == capacity, count_ref[k].astype(F32), asked)
        levels = split3(jnp.broadcast_to(level_ref[pl.ds(k, 1), :], (EXTRA, lanes)))
        sums = split3(jnp.full((EXTRA, lanes), fsum_ref[k], F32))
        rows = asked
        for at, part in enumerate(levels + sums):
            rows = jnp.where(row == at + 1, part.astype(F32), rows)
        out_ref[n, width_dom:] = rows.astype(BF16)


def pack(tables, coef, place, groups, capacity):
    inv, lead, request, fsum, count, level = tables
    _, width_dom, width_pno = coef.shape
    each = 4
    extra = 0 if place else EXTRA
    block = (1, width_dom, width_pno)

    def source(n):
        return pl.BlockSpec(block, lambda g, inv, *_: (inv[place * groups + g * each + n], 0, 0))

    return pl.pallas_call(
        functools.partial(pack_kernel, capacity, each),
        out_shape=jax.ShapeDtypeStruct((groups, width_dom + extra, width_pno), BF16),
        grid_spec=pltpu.PrefetchScalarGridSpec(
            num_scalar_prefetch=5,
            grid=(groups // each,),
            in_specs=[pl.BlockSpec(level.shape, lambda g, *_: (0, 0))]
            + [source(n) for n in range(each)],
            out_specs=pl.BlockSpec((each, width_dom + extra, width_pno), lambda g, *_: (g, 0, 0)),
        ),
        compiler_params=params(),
        cost_estimate=cost(0, 4 * groups * width_dom * width_pno),
        name="pack",
    )(inv, lead, request, fsum, count, level, *([coef] * each))


def project_kernel(columns, arrived_ref, *refs):
    out_ref = refs[-1]
    for n in range(len(refs) // 2):
        rows = lax.dot_general(
            refs[2 * n][0], refs[2 * n + 1][0], (((0,), (0,)), ((), ())), preferred_element_type=F32
        ).astype(BF16)
        spread(out_ref.at[0, pl.ds(n * columns, columns)], rows)


def project(arrived, coefs, three_index, places):
    groups, _, width_pno = coefs[0].shape
    _, width_dom, width_aux = three_index.shape
    columns = width_aux // width_pno
    specs, operands = [], []
    for place in places:
        specs.append(pl.BlockSpec((1, width_dom, width_pno), lambda g, want: (g, 0, 0)))
        specs.append(
            pl.BlockSpec(
                (1, width_dom, width_aux),
                lambda g, want, place=place: (jnp.maximum(want[g, place] - 1, 0), 0, 0),
            )
        )
        operands += [coefs[place], three_index]
    count = len(places)
    return pl.pallas_call(
        functools.partial(project_kernel, columns),
        out_shape=jax.ShapeDtypeStruct((groups, count * columns, width_pno, width_pno), BF16),
        grid_spec=pltpu.PrefetchScalarGridSpec(
            num_scalar_prefetch=1,
            grid=(groups,),
            in_specs=specs,
            out_specs=pl.BlockSpec(
                (1, count * columns, width_pno, width_pno), lambda g, want: (g, 0, 0, 0)
            ),
        ),
        compiler_params=params(),
        cost_estimate=cost(
            2 * count * groups * width_dom * width_pno * width_aux,
            2 * count * groups * (width_dom + width_pno) * width_aux,
        ),
        name="project",
    )(arrived, *operands)


def project_lanes_kernel(groups, me_ref, arrived_ref, coef_ref, block_ref, own_ref, *refs):
    lanes, (buf, sem) = refs[:-2], refs[-2:]
    r = pl.program_id(0)
    par = lax.rem(r, 2)
    rows = lax.dot_general(
        coef_ref[0], block_ref[0], (((0,), (0,)), ((), ())), preferred_element_type=F32
    ).astype(BF16)
    spread(own_ref.at[0], rows)

    def drain(which):
        pltpu.make_async_copy(buf.at[which], lanes[0], sem.at[which]).wait()

    @pl.when(r >= 2)
    def _():
        drain(par)

    spread(buf.at[par], rows)
    for n, ref in enumerate(lanes):

        @pl.when(r == n)
        def _():
            pltpu.make_async_copy(buf.at[par], ref, sem.at[par]).start()

    @pl.when(r == groups - 1)
    def _():
        drain(1 - par)
        drain(par)


def project_lanes(me, arrived, coef, three_index):
    groups, _, width_pno = coef.shape
    _, width_dom, width_aux = three_index.shape
    columns = width_aux // width_pno
    shape = (columns, width_pno, width_pno)
    own, *lanes = pl.pallas_call(
        functools.partial(project_lanes_kernel, groups),
        out_shape=[jax.ShapeDtypeStruct((groups,) + shape, BF16)]
        + [jax.ShapeDtypeStruct(shape, BF16)] * groups,
        grid_spec=pltpu.PrefetchScalarGridSpec(
            num_scalar_prefetch=2,
            grid=(groups,),
            in_specs=[
                pl.BlockSpec((1, width_dom, width_pno), lambda r, me, want: (me[0] ^ r, 0, 0)),
                pl.BlockSpec(
                    (1, width_dom, width_aux),
                    lambda r, me, want: (jnp.maximum(want[me[0] ^ r, 0] - 1, 0), 0, 0),
                ),
            ],
            out_specs=[pl.BlockSpec((1,) + shape, lambda r, me, want: (me[0] ^ r, 0, 0, 0))]
            + [ANY] * groups,
            scratch_shapes=[pltpu.VMEM((2,) + shape, BF16), pltpu.SemaphoreType.DMA((2,))],
        ),
        compiler_params=params(),
        cost_estimate=cost(
            2 * groups * width_dom * width_pno * width_aux,
            2 * groups * (width_dom + 2 * width_pno) * width_aux,
        ),
        name="project_lanes",
    )(me, arrived, coef, three_index)
    return own, lanes


def partner(me, r, groups):
    return r if groups & (groups - 1) else me ^ r


def split_slot(groups, slot):
    place = slot // groups
    return place, slot - place * groups


def fetch_slot(groups, me, slot, first, rest, buf, sem):
    place, owner = split_slot(groups, slot)
    columns = buf.shape[0]

    if len(first) == 1:

        @pl.when(place == 0)
        def _():
            pltpu.make_async_copy(first[0].at[owner], buf, sem).start()

    else:
        partner = jnp.where(place == 0, owner ^ me, -1)
        for r, ref in enumerate(first):

            @pl.when(partner == r)
            def _():
                pltpu.make_async_copy(ref, buf, sem).start()

    @pl.when(place > 0)
    def _():
        at = pl.ds((place - 1) * columns, columns)
        pltpu.make_async_copy(rest.at[owner, at], buf, sem).start()


def wait_slot(rest, buf, sem):
    pltpu.make_async_copy(rest.at[0, pl.ds(0, buf.shape[0])], buf, sem).wait()


def stream_rows(groups, me, slot_ref, first, rest, buf, sem):
    k = pl.program_id(0)
    pairs = pl.num_programs(0)
    depth = buf.shape[0]
    par = lax.rem(k, depth)

    def fetch(which, at):
        for side in range(2):
            slot = slot_ref[2 * which + side]
            fetch_slot(groups, me, slot, first, rest, buf.at[at, side], sem.at[at, side])

    @pl.when(k == 0)
    def _():
        for ahead in range(depth - 1):
            fetch(ahead, ahead)

    @pl.when(k + depth - 1 < pairs)
    def _():
        fetch(k + depth - 1, lax.rem(k + depth - 1, depth))

    for side in range(2):
        wait_slot(rest, buf.at[par, side], sem.at[par, side])
    return k, par


def relay_kernel(groups, me_ref, lead_ref, slot_ref, rest, *refs):
    first, (lanes, (buf, insem, outsem)) = refs[: -groups - 3], (refs[-groups - 3 : -3], refs[-3:])
    me = me_ref[0]

    @pl.loop(0, groups)
    def _(r):
        half = lead_ref[partner(me, r, groups)]
        fetch_slot(groups, me, slot_ref[half ^ 1], first, rest, buf.at[r], insem.at[r])

    def outward(r):
        return pltpu.make_async_copy(buf.at[r], lanes[r], outsem.at[r])

    for r in range(groups):
        wait_slot(rest, buf.at[r], insem.at[r])
        outward(r).start()
    for r in range(groups):
        outward(r).wait()


def relay(me, lead, slot_of, first, rest, columns):
    groups, _, width_pno, _ = rest.shape
    shape = (columns, width_pno, width_pno)
    return pl.pallas_call(
        functools.partial(relay_kernel, groups),
        out_shape=[jax.ShapeDtypeStruct(shape, BF16)] * groups,
        in_specs=[SMEM] * 3 + [ANY] * (1 + len(first)),
        out_specs=[ANY] * groups,
        scratch_shapes=[
            pltpu.VMEM((groups,) + shape, BF16),
            pltpu.SemaphoreType.DMA((groups,)),
            pltpu.SemaphoreType.DMA((groups,)),
        ],
        compiler_params=params(),
        cost_estimate=cost(0, 4 * groups * columns * width_pno * width_pno),
        name="relay",
    )(me, lead, slot_of, rest, *first)


def couple_kernel(groups, me_ref, slot_ref, rest, *refs):
    first, (out_ref, buf, sem) = refs[:-3], refs[-3:]
    _, par = stream_rows(groups, me_ref[0], slot_ref, first, rest, buf, sem)
    out_ref[0] = lax.dot_general(
        wide(buf.at[par, 0]),
        wide(buf.at[par, 1]),
        (((1,), (1,)), ((), ())),
        preferred_element_type=F32,
    ).astype(out_ref.dtype)


def couple(me, slot_of, first, rest, pairs, columns, dtype):
    groups, _, width_pno, _ = rest.shape
    depth = min(4, pairs)
    moved = pairs * columns * width_pno * width_pno
    return pl.pallas_call(
        functools.partial(couple_kernel, groups),
        out_shape=jax.ShapeDtypeStruct((pairs, width_pno, width_pno), dtype),
        grid_spec=pltpu.PrefetchScalarGridSpec(
            num_scalar_prefetch=2,
            grid=(pairs,),
            in_specs=[ANY] * (1 + len(first)),
            out_specs=pl.BlockSpec((1, width_pno, width_pno), lambda k, *_: (k, 0, 0)),
            scratch_shapes=[
                pltpu.VMEM((depth, 2, columns, width_pno, width_pno), BF16),
                pltpu.SemaphoreType.DMA((depth, 2)),
            ],
        ),
        compiler_params=params(),
        cost_estimate=cost(2 * moved * width_pno, 4 * moved),
        name="couple",
    )(me, slot_of, rest, *first)


def amplitudes(coupling, levels, fsum, count):
    width = coupling.shape[0]
    across = jnp.broadcast_to(levels, (width, width))
    denom = across.T + across - fsum
    inside = (lax.broadcasted_iota(I32, (width, width), 0) < count) & (
        lax.broadcasted_iota(I32, (width, width), 1) < count
    )
    return jnp.where(inside, -coupling / denom, jnp.float32(0.0))


def total(partial):
    coupling = partial[0][0].astype(F32)
    for extra in partial[1:]:
        coupling = coupling + extra[0].astype(F32)
    return coupling


def weigh_kernel(groups, parts, me_ref, slot_ref, home_ref, count_ref, fsum_ref, *refs):
    partial = refs[:parts]
    level_ref, rest = refs[parts : parts + 2]
    first, outs = refs[parts + 2 : -6], refs[-6:]
    gamma_ref, energy_ref, buf, sem, outbuf, outsem = outs
    k, par = stream_rows(groups, me_ref[0], slot_ref, first, rest, buf, sem)
    pairs = pl.num_programs(0)
    columns = buf.shape[2]
    coupling = total(partial)
    amplitude = amplitudes(coupling, level_ref[pl.ds(k, 1), :], fsum_ref[k], count_ref[k])
    turned = amplitude.T
    mixed = 2.0 * amplitude - turned
    energy_ref[pl.ds(k, 1), :] = jnp.sum(coupling * mixed, axis=0, keepdims=True)
    weights = (mixed.astype(BF16), (2.0 * turned - amplitude).astype(BF16))
    half = lax.rem(k, 2)

    def send(which, buffer, go):
        for side in range(2):
            place, owner = split_slot(groups, home_ref[2 * which + side])

            @pl.when(place > 0)
            def _():
                at = pl.ds((place - 1) * columns, columns)
                go(
                    pltpu.make_async_copy(
                        outbuf.at[buffer, side], gamma_ref.at[owner, at], outsem.at[buffer, side]
                    )
                )

    @pl.when(k >= 2)
    def _():
        send(k - 2, half, lambda copy: copy.wait())

    for side in range(2):
        spread(
            outbuf.at[half, side],
            jnp.dot(
                weights[side], wide(buf.at[par, 1 - side]), preferred_element_type=F32
            ).astype(BF16),
        )
    send(k, half, lambda copy: copy.start())

    @pl.when(k == pairs - 1)
    def _():
        @pl.when(k >= 1)
        def _():
            send(k - 1, 1 - half, lambda copy: copy.wait())

        send(k, half, lambda copy: copy.wait())


def weigh(me, slot_of, home, count, fsum, partial, level, first, rest, columns):
    groups, _, width_pno, _ = rest.shape
    pairs = level.shape[0]
    depth = min(3, pairs)
    moved = pairs * columns * width_pno * width_pno
    return pl.pallas_call(
        functools.partial(weigh_kernel, groups, len(partial)),
        out_shape=(
            jax.ShapeDtypeStruct(rest.shape, BF16),
            jax.ShapeDtypeStruct((pairs, width_pno), F32),
        ),
        grid_spec=pltpu.PrefetchScalarGridSpec(
            num_scalar_prefetch=5,
            grid=(pairs,),
            in_specs=[
                pl.BlockSpec((1, width_pno, width_pno), lambda k, *_: (k, 0, 0)) for _ in partial
            ]
            + [pl.BlockSpec((pairs, width_pno), lambda k, *_: (0, 0))]
            + [ANY] * (1 + len(first)),
            out_specs=(ANY, pl.BlockSpec((pairs, width_pno), lambda k, *_: (0, 0))),
            scratch_shapes=[
                pltpu.VMEM((depth, 2, columns, width_pno, width_pno), BF16),
                pltpu.SemaphoreType.DMA((depth, 2)),
                pltpu.VMEM((2, 2, columns, width_pno, width_pno), BF16),
                pltpu.SemaphoreType.DMA((2, 2)),
            ],
        ),
        compiler_params=params(),
        cost_estimate=cost(4 * width_pno * moved, 8 * moved),
        name="weigh",
    )(me, slot_of, home, count, fsum, *partial, level, rest, *first)


def couple_here_kernel(me_ref, flip_ref, *refs):
    owned, (other_ref, out_ref) = refs[:-2], refs[-2:]
    own = wide(owned[0].at[0])
    for ref in owned[1:]:
        own = jnp.where(flip_ref[0] == 0, own, wide(ref.at[0]))
    out_ref[0] = lax.dot_general(
        own, wide(other_ref.at[0]), (((1,), (1,)), ((), ())), preferred_element_type=F32
    ).astype(out_ref.dtype)


def couple_here(me, flip, owned, other, dtype):
    groups, columns, width_pno, _ = other.shape
    block = (1, columns, width_pno, width_pno)

    def mine(r, me, flip):
        return (partner(me[0], r, groups), 0, 0, 0)

    return pl.pallas_call(
        couple_here_kernel,
        out_shape=jax.ShapeDtypeStruct((groups, width_pno, width_pno), dtype),
        grid_spec=pltpu.PrefetchScalarGridSpec(
            num_scalar_prefetch=2,
            grid=(groups,),
            in_specs=[pl.BlockSpec(block, mine)] * len(owned)
            + [pl.BlockSpec(block, lambda r, me, flip: (r, 0, 0, 0))],
            out_specs=pl.BlockSpec((1, width_pno, width_pno), lambda r, me, flip: (r, 0, 0)),
        ),
        compiler_params=params(),
        cost_estimate=cost(2 * other.size * width_pno, 4 * other.size),
        name="couple_here",
    )(me, flip, *owned, other)


def weigh_here_kernel(capacity, parts, me_ref, *refs):
    partial = refs[:parts]
    facts_ref, rows_ref, out_ref = refs[parts:]
    facts = facts_ref[0].astype(F32)
    levels = join3(facts[1:2], facts[2:3], facts[3:4])
    fsum = join3(facts[4:5], facts[5:6], facts[6:7])
    count = facts[0:1, capacity : capacity + 1].astype(I32)
    amplitude = amplitudes(total(partial), levels, fsum, count)
    weights = (2.0 * amplitude - amplitude.T).astype(BF16)
    spread(
        out_ref.at[0],
        jnp.dot(weights, wide(rows_ref.at[0]), preferred_element_type=F32).astype(BF16),
    )


def weigh_here(me, partial, coef, rows, width_dom, capacity):
    groups, columns, width_pno, _ = rows.shape
    square = pl.BlockSpec((1, width_pno, width_pno), lambda r, me: (r, 0, 0))
    block = pl.BlockSpec((1, columns, width_pno, width_pno), lambda r, me: (r, 0, 0, 0))
    facts = pl.BlockSpec(
        (1, EXTRA, width_pno),
        lambda r, me: (partner(me[0], r, groups), width_dom // EXTRA, 0),
    )
    return pl.pallas_call(
        functools.partial(weigh_here_kernel, capacity, len(partial)),
        out_shape=jax.ShapeDtypeStruct(rows.shape, BF16),
        grid_spec=pltpu.PrefetchScalarGridSpec(
            num_scalar_prefetch=1,
            grid=(groups,),
            in_specs=[square] * len(partial) + [facts, block],
            out_specs=block,
        ),
        compiler_params=params(),
        cost_estimate=cost(2 * rows.size * width_pno, 4 * rows.size),
        name="weigh_here",
    )(me, *partial, coef, rows)


def lay_kernel(groups, places, order_ref, *refs):
    out_ref = refs[-1]
    u = pl.program_id(0)
    width_pno = out_ref.shape[2] // 2
    for n in range(2):
        slot = order_ref[2 * u + n]
        place = jnp.where(slot < 0, -1, slot // groups)
        value = jnp.zeros(out_ref.shape[1:2] + (width_pno,), BF16)
        for c in range(places):
            value = jnp.where(place == c, refs[n * places + c][0], value)
        out_ref[0, :, n * width_pno : (n + 1) * width_pno] = value


def lay_coefs(order, coefs, width_dom):
    groups, _, width_pno = coefs[0].shape
    steps = order.shape[0] // 2

    def source(n):
        return pl.BlockSpec(
            (1, width_dom, width_pno),
            lambda u, order: (lax.rem(jnp.maximum(order[2 * u + n], 0), groups), 0, 0),
        )

    places = len(coefs)
    return pl.pallas_call(
        functools.partial(lay_kernel, groups, places),
        out_shape=jax.ShapeDtypeStruct((steps, width_dom, 2 * width_pno), BF16),
        grid_spec=pltpu.PrefetchScalarGridSpec(
            num_scalar_prefetch=1,
            grid=(steps,),
            in_specs=[source(n) for n in range(2) for _ in coefs],
            out_specs=pl.BlockSpec((1, width_dom, 2 * width_pno), lambda u, order: (u, 0, 0)),
        ),
        compiler_params=params(),
        cost_estimate=cost(0, 20 * steps * width_dom * width_pno),
        name="lay_coefs",
    )(order, *coefs, *coefs)


def gather_kernel(groups, me_ref, flip_ref, order_ref, start_ref, rows_ref, gamma_ref, *refs):
    left_ref, out_ref, gbuf, gsem, cbuf, csem = refs
    o = pl.program_id(0)
    couples = start_ref[pl.num_programs(0)] // 2
    depth = gbuf.shape[0]

    def fetch(u):
        at = lax.rem(u, depth)
        pltpu.make_async_copy(left_ref.at[u], cbuf.at[at], csem.at[at]).start()
        lone = order_ref[2 * u]
        for n in range(2):
            slot = order_ref[2 * u + n]
            slot = jnp.where(slot < 0, lone, slot)
            place, owner = split_slot(groups, slot)
            rank = place ^ flip_ref[0]
            lane = partner(me_ref[0], owner, groups)
            home = rank * groups + jnp.where(rank == 0, lane, owner)
            fetch_slot(groups, 0, home, [rows_ref], gamma_ref, gbuf.at[at, n], gsem.at[at, n])

    @pl.when(o == 0)
    def _():
        for u in range(depth - 1):

            @pl.when(u < couples)
            def _():
                fetch(u)

    begin, end = start_ref[o] // 2, start_ref[o + 1] // 2

    @pl.when(begin == end)
    def _():
        out_ref[...] = jnp.zeros_like(out_ref)

    def step(u, fresh):
        @pl.when(u + depth - 1 < couples)
        def _():
            fetch(u + depth - 1)

        at = lax.rem(u, depth)
        pltpu.make_async_copy(left_ref.at[0], cbuf.at[at], csem.at[at]).wait()
        for n in range(2):
            wait_slot(gamma_ref, gbuf.at[at, n], gsem.at[at, n])
        columns, lanes = gbuf.shape[2], gbuf.shape[4]
        each = 2 - columns % 2
        for j in range(0, columns, each):
            right = jnp.concatenate(
                [wide(gbuf.at[at, n, pl.ds(j, each)]) for n in range(2)], axis=0
            )
            value = jnp.dot(cbuf[at], right, preferred_element_type=F32)
            where = pl.ds(j * lanes, each * lanes)
            out_ref[0, :, where] = value if fresh else out_ref[0, :, where] + value

    @pl.when(begin < end)
    def _():
        step(begin, True)

    @pl.loop(begin + 1, end)
    def _(u):
        step(u, False)


def gather_terms(me, flip, order, start, rows, gamma, left, occ_dev):
    groups, columns, width_pno, _ = rows.shape
    width_aux = columns * width_pno
    steps, width_dom, _ = left.shape
    depth = 5
    return pl.pallas_call(
        functools.partial(gather_kernel, groups),
        out_shape=jax.ShapeDtypeStruct((occ_dev, width_dom, width_aux), F32),
        grid_spec=pltpu.PrefetchScalarGridSpec(
            num_scalar_prefetch=4,
            grid=(occ_dev,),
            in_specs=[ANY] * 3,
            out_specs=pl.BlockSpec((1, width_dom, width_aux), lambda o, *_: (o, 0, 0)),
            scratch_shapes=[
                pltpu.VMEM((depth, 2, columns, width_pno, width_pno), BF16),
                pltpu.SemaphoreType.DMA((depth, 2)),
                pltpu.VMEM((depth, width_dom, 2 * width_pno), BF16),
                pltpu.SemaphoreType.DMA((depth,)),
            ],
        ),
        compiler_params=params(),
        cost_estimate=cost(
            4 * steps * width_dom * width_pno * width_aux,
            4 * steps * width_pno * width_aux + 4 * occ_dev * width_dom * width_aux,
        ),
        name="gather_terms",
    )(me, flip, order, start, rows, gamma, left)


def exchange(x):
    return lax.all_to_all(x, "pair", split_axis=0, concat_axis=0, tiled=True)


def crossed(lanes):
    groups = len(lanes)
    lanes = list(lanes)
    for r in reversed(range(1, groups)):
        lanes[r] = lax.ppermute(lanes[r], "pair", [(i, i ^ r) for i in range(groups)])
    return lanes


def swap(x):
    return lax.ppermute(x, "aux", [(0, 1), (1, 0)])


def body(three_index, fock_diag, pair_occ, pno_count, pno_energy, pno_coef):
    groups = lax.axis_size("pair")
    twins = lax.axis_size("aux") == 2
    occ_dev, width_dom, _ = three_index.shape
    pairs = pair_occ.shape[0]
    width_pno = pno_coef.shape[3]
    halves = 2 * pairs
    capacity = max(2, halves // groups + 1)
    capacity += capacity % 2
    flip = (lax.axis_index("aux") if twins else jnp.int32(0)).astype(I32).reshape(1)
    slot_of, home, inv, lead, request, fsum = index_tables(
        flip, pair_occ, fock_diag, occ_dev, groups, capacity
    )
    coef_half = pno_coef.reshape(halves, width_dom, width_pno)
    tables = (inv, lead, request, fsum, pno_count, pno_energy)
    coefs = []
    for place in range(capacity):
        if twins and place % 2:
            coefs.append(swap(coefs[-1]))
        else:
            packed = pack(tables, coef_half, place, groups, capacity)
            coefs.append(exchange(packed))
    arrived = coefs[0][:, width_dom, :capacity].astype(F32).astype(I32)
    columns = three_index.shape[2] // width_pno
    me = lax.axis_index("pair").astype(I32).reshape(1)
    if groups & (groups - 1):
        own = project(arrived, coefs, three_index, (0,))
        first = [exchange(own)]
    else:
        own, first = project_lanes(me, arrived, coefs[0], three_index)
        first = crossed(first)
    own_rest = project(arrived, coefs, three_index, tuple(range(1, capacity)))
    rest = exchange(own_rest)
    relayed = relay(me, lead, slot_of, first, rest, columns)
    if groups & (groups - 1):
        relayed = exchange(jnp.stack(relayed))
    else:
        relayed = crossed(relayed)
    rounded = BF16 if twins else F32

    def complete(mine):
        return [mine, swap(mine)] if twins else [lax.psum(mine, "aux")]

    mine = couple(me, slot_of, first, rest, pairs, columns, rounded)
    partial = complete(mine)
    gamma, energy = weigh(
        me, slot_of, home, pno_count, fsum, partial, pno_energy, first, rest, columns
    )
    gamma = exchange(gamma)
    order, start = order_tables(arrived, occ_dev)
    if isinstance(relayed, list):
        relayed = jnp.stack(relayed)
    partial = complete(couple_here(me, flip, [own, own_rest] if twins else [own], relayed, rounded))
    relayed = weigh_here(me, partial, coefs[0], relayed, width_dom, capacity)
    left = lay_coefs(order, coefs, width_dom)
    grad = gather_terms(me, flip, order, start, relayed, gamma, left, occ_dev)
    return jnp.sum(energy, axis=1) / (width_pno * width_pno), grad


def solution(mesh):
    placed = (
        P("pair", None, "aux"),
        P(),
        P("pair", None),
        P("pair"),
        P("pair", None),
        P("pair", None, None, None),
    )
    return jax.shard_map(
        body,
        mesh=mesh,
        in_specs=placed,
        out_specs=(P("pair"), P("pair", None, "aux")),
        check_vma=False,
    )
```

```python
import functools

import jax
import jax.numpy as jnp
from jax import lax
from jax.experimental import pallas as pl
from jax.experimental.pallas import tpu as pltpu
from jax.sharding import PartitionSpec as P


F32, BF16, I32 = jnp.float32, jnp.bfloat16, jnp.int32
ANY = pl.BlockSpec(memory_space=pl.ANY)
SMEM = pl.BlockSpec(memory_space=pltpu.SMEM)
EXTRA = 16


def params():
    return pltpu.CompilerParams()


def cost(flops, moved):
    return pl.CostEstimate(flops=int(flops), bytes_accessed=int(moved), transcendentals=0)


def index_kernel(occ_dev, groups, capacity, *refs):
    flip_ref, occ_ref, fock_ref, slot_ref, home_ref, inv_ref, lead_ref, req_ref, fsum_ref, seen = refs
    pairs = occ_ref.shape[0]
    flip = flip_ref[0]

    @pl.loop(0, groups)
    def _(g):
        seen[g] = 0
        lead_ref[g] = 0

    @pl.loop(0, groups * capacity)
    def _(s):
        inv_ref[s] = 0
        req_ref[s] = 0

    @pl.loop(0, pairs)
    def _(k):
        total = jnp.float32(0.0)
        for side in range(2):
            occ = occ_ref[k, side]
            owner = occ // occ_dev
            rank = seen[owner]
            seen[owner] = rank + 1
            place = rank ^ flip
            slot = place * groups + owner
            slot_ref[2 * k + side] = slot
            home_ref[2 * k + side] = rank * groups + owner
            inv_ref[slot] = 2 * k + side

            @pl.when(rank == 0)
            def _():
                lead_ref[owner] = 2 * k + side

            req_ref[owner * capacity + place] = occ - owner * occ_dev + 1
            total = total + fock_ref[occ]
        fsum_ref[k] = total


def index_tables(flip, pair_occ, fock_diag, occ_dev, groups, capacity):
    pairs = pair_occ.shape[0]
    slots = groups * capacity
    return pl.pallas_call(
        functools.partial(index_kernel, occ_dev, groups, capacity),
        out_shape=(
            jax.ShapeDtypeStruct((2 * pairs,), I32),
            jax.ShapeDtypeStruct((2 * pairs,), I32),
            jax.ShapeDtypeStruct((slots,), I32),
            jax.ShapeDtypeStruct((groups,), I32),
            jax.ShapeDtypeStruct((slots,), I32),
            jax.ShapeDtypeStruct((pairs,), F32),
        ),
        in_specs=[SMEM] * 3,
        out_specs=(SMEM,) * 6,
        scratch_shapes=[pltpu.SMEM((groups,), I32)],
        name="index_tables",
    )(flip, pair_occ, fock_diag)


def order_kernel(occ_dev, groups, capacity, arrived_ref, order_ref, start_ref, fill):
    @pl.loop(0, occ_dev)
    def _(o):
        fill[o] = 0

    @pl.loop(0, order_ref.shape[0])
    def _(t):
        order_ref[t] = -1

    @pl.loop(0, groups)
    def _(g):
        for place in range(capacity):
            want = arrived_ref[g, place]

            @pl.when(want > 0)
            def _():
                fill[want - 1] = fill[want - 1] + 1

    def running(o, total):
        count = fill[o]
        start_ref[o] = total
        fill[o] = total
        return total + 2 * ((count + 1) // 2)

    start_ref[occ_dev] = lax.fori_loop(0, occ_dev, running, jnp.int32(0))

    @pl.loop(0, groups)
    def _(g):
        for place in range(capacity):
            want = arrived_ref[g, place]

            @pl.when(want > 0)
            def _():
                at = fill[want - 1]
                order_ref[at] = place * groups + g
                fill[want - 1] = at + 1


def order_tables(arrived, occ_dev):
    groups, capacity = arrived.shape
    return pl.pallas_call(
        functools.partial(order_kernel, occ_dev, groups, capacity),
        out_shape=(
            jax.ShapeDtypeStruct((groups * capacity + occ_dev,), I32),
            jax.ShapeDtypeStruct((occ_dev + 1,), I32),
        ),
        in_specs=[SMEM],
        out_specs=(SMEM, SMEM),
        scratch_shapes=[pltpu.SMEM((occ_dev,), I32)],
        name="order_tables",
    )(arrived)


def wide(ref):
    return jnp.concatenate([ref[j] for j in range(ref.shape[0])], axis=1)


def spread(ref, value):
    lanes = ref.shape[2]
    for j in range(ref.shape[0]):
        ref[j] = value[:, j * lanes : (j + 1) * lanes]


def split3(x):
    high = x.astype(BF16)
    left = x - high.astype(F32)
    middle = left.astype(BF16)
    return high, middle, (left - middle.astype(F32)).astype(BF16)


def join3(high, middle, low):
    return (high.astype(F32) + middle.astype(F32)) + low.astype(F32)


def pack_kernel(capacity, each, inv_ref, lead_ref, req_ref, fsum_ref, count_ref, level_ref, *refs):
    out_ref = refs[-1]
    width_dom, lanes = refs[0].shape[1:]
    for n, ref in enumerate(refs[:-1]):
        out_ref[n, :width_dom] = ref[0]
        if out_ref.shape[1] == width_dom:
            continue
        g = pl.program_id(0) * each + n
        k = lead_ref[g] // 2
        row = lax.broadcasted_iota(I32, (EXTRA, lanes), 0)
        lane = lax.broadcasted_iota(I32, (EXTRA, lanes), 1)
        asked = jnp.zeros((EXTRA, lanes), F32)
        for v in range(capacity):
            asked = jnp.where(lane == v, req_ref[g * capacity + v].astype(F32), asked)
        asked = jnp.where(lane == capacity, count_ref[k].astype(F32), asked)
        levels = split3(jnp.broadcast_to(level_ref[pl.ds(k, 1), :], (EXTRA, lanes)))
        sums = split3(jnp.full((EXTRA, lanes), fsum_ref[k], F32))
        rows = asked
        for at, part in enumerate(levels + sums):
            rows = jnp.where(row == at + 1, part.astype(F32), rows)
        out_ref[n, width_dom:] = rows.astype(BF16)


def pack(tables, coef, place, groups, capacity):
    inv, lead, request, fsum, count, level = tables
    _, width_dom, width_pno = coef.shape
    each = 8
    extra = 0 if place else EXTRA
    block = (1, width_dom, width_pno)

    def source(n):
        return pl.BlockSpec(block, lambda g, inv, *_: (inv[place * groups + g * each + n], 0, 0))

    return pl.pallas_call(
        functools.partial(pack_kernel, capacity, each),
        out_shape=jax.ShapeDtypeStruct((groups, width_dom + extra, width_pno), BF16),
        grid_spec=pltpu.PrefetchScalarGridSpec(
            num_scalar_prefetch=5,
            grid=(groups // each,),
            in_specs=[pl.BlockSpec(level.shape, lambda g, *_: (0, 0))]
            + [source(n) for n in range(each)],
            out_specs=pl.BlockSpec((each, width_dom + extra, width_pno), lambda g, *_: (g, 0, 0)),
        ),
        compiler_params=params(),
        cost_estimate=cost(0, 4 * groups * width_dom * width_pno),
        name="pack",
    )(inv, lead, request, fsum, count, level, *([coef] * each))


def project_kernel(columns, arrived_ref, *refs):
    out_ref = refs[-1]
    for n in range(len(refs) // 2):
        rows = lax.dot_general(
            refs[2 * n][0], refs[2 * n + 1][0], (((0,), (0,)), ((), ())), preferred_element_type=F32
        ).astype(BF16)
        spread(out_ref.at[0, pl.ds(n * columns, columns)], rows)


def project(arrived, coefs, three_index, places):
    groups, _, width_pno = coefs[0].shape
    _, width_dom, width_aux = three_index.shape
    columns = width_aux // width_pno
    specs, operands = [], []
    for place in places:
        specs.append(pl.BlockSpec((1, width_dom, width_pno), lambda g, want: (g, 0, 0)))
        specs.append(
            pl.BlockSpec(
                (1, width_dom, width_aux),
                lambda g, want, place=place: (jnp.maximum(want[g, place] - 1, 0), 0, 0),
            )
        )
        operands += [coefs[place], three_index]
    count = len(places)
    return pl.pallas_call(
        functools.partial(project_kernel, columns),
        out_shape=jax.ShapeDtypeStruct((groups, count * columns, width_pno, width_pno), BF16),
        grid_spec=pltpu.PrefetchScalarGridSpec(
            num_scalar_prefetch=1,
            grid=(groups,),
            in_specs=specs,
            out_specs=pl.BlockSpec(
                (1, count * columns, width_pno, width_pno), lambda g, want: (g, 0, 0, 0)
            ),
        ),
        compiler_params=params(),
        cost_estimate=cost(
            2 * count * groups * width_dom * width_pno * width_aux,
            2 * count * groups * (width_dom + width_pno) * width_aux,
        ),
        name="project",
    )(arrived, *operands)


def project_lanes_kernel(groups, me_ref, arrived_ref, coef_ref, block_ref, own_ref, *refs):
    lanes, (buf, sem) = refs[:-2], refs[-2:]
    r = pl.program_id(0)
    par = lax.rem(r, 2)
    rows = lax.dot_general(
        coef_ref[0], block_ref[0], (((0,), (0,)), ((), ())), preferred_element_type=F32
    ).astype(BF16)
    spread(own_ref.at[0], rows)

    def drain(which):
        pltpu.make_async_copy(buf.at[which], lanes[0], sem.at[which]).wait()

    @pl.when(r >= 2)
    def _():
        drain(par)

    spread(buf.at[par], rows)
    for n, ref in enumerate(lanes):

        @pl.when(r == n)
        def _():
            pltpu.make_async_copy(buf.at[par], ref, sem.at[par]).start()

    @pl.when(r == groups - 1)
    def _():
        drain(1 - par)
        drain(par)


def project_lanes(me, arrived, coef, three_index):
    groups, _, width_pno = coef.shape
    _, width_dom, width_aux = three_index.shape
    columns = width_aux // width_pno
    shape = (columns, width_pno, width_pno)
    own, *lanes = pl.pallas_call(
        functools.partial(project_lanes_kernel, groups),
        out_shape=[jax.ShapeDtypeStruct((groups,) + shape, BF16)]
        + [jax.ShapeDtypeStruct(shape, BF16)] * groups,
        grid_spec=pltpu.PrefetchScalarGridSpec(
            num_scalar_prefetch=2,
            grid=(groups,),
            in_specs=[
                pl.BlockSpec((1, width_dom, width_pno), lambda r, me, want: (me[0] ^ r, 0, 0)),
                pl.BlockSpec(
                    (1, width_dom, width_aux),
                    lambda r, me, want: (jnp.maximum(want[me[0] ^ r, 0] - 1, 0), 0, 0),
                ),
            ],
            out_specs=[pl.BlockSpec((1,) + shape, lambda r, me, want: (me[0] ^ r, 0, 0, 0))]
            + [ANY] * groups,
            scratch_shapes=[pltpu.VMEM((2,) + shape, BF16), pltpu.SemaphoreType.DMA((2,))],
        ),
        compiler_params=params(),
        cost_estimate=cost(
            2 * groups * width_dom * width_pno * width_aux,
            2 * groups * (width_dom + 2 * width_pno) * width_aux,
        ),
        name="project_lanes",
    )(me, arrived, coef, three_index)
    return own, lanes


def partner(me, r, groups):
    return r if groups & (groups - 1) else me ^ r


def split_slot(groups, slot):
    place = slot // groups
    return place, slot - place * groups


def fetch_slot(groups, me, slot, first, rest, buf, sem):
    place, owner = split_slot(groups, slot)
    columns = buf.shape[0]

    if len(first) == 1:

        @pl.when(place == 0)
        def _():
            pltpu.make_async_copy(first[0].at[owner], buf, sem).start()

    else:
        partner = jnp.where(place == 0, owner ^ me, -1)
        for r, ref in enumerate(first):

            @pl.when(partner == r)
            def _():
                pltpu.make_async_copy(ref, buf, sem).start()

    @pl.when(place > 0)
    def _():
        at = pl.ds((place - 1) * columns, columns)
        pltpu.make_async_copy(rest.at[owner, at], buf, sem).start()


def wait_slot(rest, buf, sem):
    pltpu.make_async_copy(rest.at[0, pl.ds(0, buf.shape[0])], buf, sem).wait()


def stream_rows(groups, me, slot_ref, first, rest, buf, sem):
    k = pl.program_id(0)
    pairs = pl.num_programs(0)
    depth = buf.shape[0]
    par = lax.rem(k, depth)

    def fetch(which, at):
        for side in range(2):
            slot = slot_ref[2 * which + side]
            fetch_slot(groups, me, slot, first, rest, buf.at[at, side], sem.at[at, side])

    @pl.when(k == 0)
    def _():
        for ahead in range(depth - 1):
            fetch(ahead, ahead)

    @pl.when(k + depth - 1 < pairs)
    def _():
        fetch(k + depth - 1, lax.rem(k + depth - 1, depth))

    for side in range(2):
        wait_slot(rest, buf.at[par, side], sem.at[par, side])
    return k, par


def relay_kernel(groups, me_ref, lead_ref, slot_ref, rest, *refs):
    first, (lanes, (buf, insem, outsem)) = refs[: -groups - 3], (refs[-groups - 3 : -3], refs[-3:])
    me = me_ref[0]

    @pl.loop(0, groups)
    def _(r):
        half = lead_ref[partner(me, r, groups)]
        fetch_slot(groups, me, slot_ref[half ^ 1], first, rest, buf.at[r], insem.at[r])

    def outward(r):
        return pltpu.make_async_copy(buf.at[r], lanes[r], outsem.at[r])

    for r in range(groups):
        wait_slot(rest, buf.at[r], insem.at[r])
        outward(r).start()
    for r in range(groups):
        outward(r).wait()


def relay(me, lead, slot_of, first, rest, columns):
    groups, _, width_pno, _ = rest.shape
    shape = (columns, width_pno, width_pno)
    return pl.pallas_call(
        functools.partial(relay_kernel, groups),
        out_shape=[jax.ShapeDtypeStruct(shape, BF16)] * groups,
        in_specs=[SMEM] * 3 + [ANY] * (1 + len(first)),
        out_specs=[ANY] * groups,
        scratch_shapes=[
            pltpu.VMEM((groups,) + shape, BF16),
            pltpu.SemaphoreType.DMA((groups,)),
            pltpu.SemaphoreType.DMA((groups,)),
        ],
        compiler_params=params(),
        cost_estimate=cost(0, 4 * groups * columns * width_pno * width_pno),
        name="relay",
    )(me, lead, slot_of, rest, *first)


def couple_kernel(groups, me_ref, slot_ref, rest, *refs):
    first, (out_ref, buf, sem) = refs[:-3], refs[-3:]
    _, par = stream_rows(groups, me_ref[0], slot_ref, first, rest, buf, sem)
    out_ref[0] = lax.dot_general(
        wide(buf.at[par, 0]),
        wide(buf.at[par, 1]),
        (((1,), (1,)), ((), ())),
        preferred_element_type=F32,
    ).astype(out_ref.dtype)


def couple(me, slot_of, first, rest, pairs, columns, dtype):
    groups, _, width_pno, _ = rest.shape
    depth = min(4, pairs)
    moved = pairs * columns * width_pno * width_pno
    return pl.pallas_call(
        functools.partial(couple_kernel, groups),
        out_shape=jax.ShapeDtypeStruct((pairs, width_pno, width_pno), dtype),
        grid_spec=pltpu.PrefetchScalarGridSpec(
            num_scalar_prefetch=2,
            grid=(pairs,),
            in_specs=[ANY] * (1 + len(first)),
            out_specs=pl.BlockSpec((1, width_pno, width_pno), lambda k, *_: (k, 0, 0)),
            scratch_shapes=[
                pltpu.VMEM((depth, 2, columns, width_pno, width_pno), BF16),
                pltpu.SemaphoreType.DMA((depth, 2)),
            ],
        ),
        compiler_params=params(),
        cost_estimate=cost(2 * moved * width_pno, 4 * moved),
        name="couple",
    )(me, slot_of, rest, *first)


def amplitudes(coupling, levels, fsum, count):
    width = coupling.shape[0]
    across = jnp.broadcast_to(levels, (width, width))
    denom = across.T + across - fsum
    inside = (lax.broadcasted_iota(I32, (width, width), 0) < count) & (
        lax.broadcasted_iota(I32, (width, width), 1) < count
    )
    return jnp.where(inside, -coupling / denom, jnp.float32(0.0))


def total(partial):
    coupling = partial[0][0].astype(F32)
    for extra in partial[1:]:
        coupling = coupling + extra[0].astype(F32)
    return coupling


def weigh_kernel(groups, parts, me_ref, slot_ref, home_ref, count_ref, fsum_ref, *refs):
    partial = refs[:parts]
    level_ref, rest = refs[parts : parts + 2]
    first, outs = refs[parts + 2 : -6], refs[-6:]
    gamma_ref, energy_ref, buf, sem, outbuf, outsem = outs
    k, par = stream_rows(groups, me_ref[0], slot_ref, first, rest, buf, sem)
    pairs = pl.num_programs(0)
    columns = buf.shape[2]
    coupling = total(partial)
    amplitude = amplitudes(coupling, level_ref[pl.ds(k, 1), :], fsum_ref[k], count_ref[k])
    turned = amplitude.T
    mixed = 2.0 * amplitude - turned
    energy_ref[pl.ds(k, 1), :] = jnp.sum(coupling * mixed, axis=0, keepdims=True)
    weights = (mixed.astype(BF16), (2.0 * turned - amplitude).astype(BF16))
    half = lax.rem(k, 2)

    def send(which, buffer, go):
        for side in range(2):
            place, owner = split_slot(groups, home_ref[2 * which + side])

            @pl.when(place > 0)
            def _():
                at = pl.ds((place - 1) * columns, columns)
                go(
                    pltpu.make_async_copy(
                        outbuf.at[buffer, side], gamma_ref.at[owner, at], outsem.at[buffer, side]
                    )
                )

    @pl.when(k >= 2)
    def _():
        send(k - 2, half, lambda copy: copy.wait())

    for side in range(2):
        spread(
            outbuf.at[half, side],
            jnp.dot(
                weights[side], wide(buf.at[par, 1 - side]), preferred_element_type=F32
            ).astype(BF16),
        )
    send(k, half, lambda copy: copy.start())

    @pl.when(k == pairs - 1)
    def _():
        @pl.when(k >= 1)
        def _():
            send(k - 1, 1 - half, lambda copy: copy.wait())

        send(k, half, lambda copy: copy.wait())


def weigh(me, slot_of, home, count, fsum, partial, level, first, rest, columns):
    groups, _, width_pno, _ = rest.shape
    pairs = level.shape[0]
    depth = min(3, pairs)
    moved = pairs * columns * width_pno * width_pno
    return pl.pallas_call(
        functools.partial(weigh_kernel, groups, len(partial)),
        out_shape=(
            jax.ShapeDtypeStruct(rest.shape, BF16),
            jax.ShapeDtypeStruct((pairs, width_pno), F32),
        ),
        grid_spec=pltpu.PrefetchScalarGridSpec(
            num_scalar_prefetch=5,
            grid=(pairs,),
            in_specs=[
                pl.BlockSpec((1, width_pno, width_pno), lambda k, *_: (k, 0, 0)) for _ in partial
            ]
            + [pl.BlockSpec((pairs, width_pno), lambda k, *_: (0, 0))]
            + [ANY] * (1 + len(first)),
            out_specs=(ANY, pl.BlockSpec((pairs, width_pno), lambda k, *_: (0, 0))),
            scratch_shapes=[
                pltpu.VMEM((depth, 2, columns, width_pno, width_pno), BF16),
                pltpu.SemaphoreType.DMA((depth, 2)),
                pltpu.VMEM((2, 2, columns, width_pno, width_pno), BF16),
                pltpu.SemaphoreType.DMA((2, 2)),
            ],
        ),
        compiler_params=params(),
        cost_estimate=cost(4 * width_pno * moved, 8 * moved),
        name="weigh",
    )(me, slot_of, home, count, fsum, *partial, level, rest, *first)


def couple_here_kernel(me_ref, flip_ref, *refs):
    owned, (other_ref, out_ref) = refs[:-2], refs[-2:]
    own = wide(owned[0].at[0])
    for ref in owned[1:]:
        own = jnp.where(flip_ref[0] == 0, own, wide(ref.at[0]))
    out_ref[0] = lax.dot_general(
        own, wide(other_ref.at[0]), (((1,), (1,)), ((), ())), preferred_element_type=F32
    ).astype(out_ref.dtype)


def couple_here(me, flip, owned, other, dtype):
    groups, columns, width_pno, _ = other.shape
    block = (1, columns, width_pno, width_pno)

    def mine(r, me, flip):
        return (partner(me[0], r, groups), 0, 0, 0)

    return pl.pallas_call(
        couple_here_kernel,
        out_shape=jax.ShapeDtypeStruct((groups, width_pno, width_pno), dtype),
        grid_spec=pltpu.PrefetchScalarGridSpec(
            num_scalar_prefetch=2,
            grid=(groups,),
            in_specs=[pl.BlockSpec(block, mine)] * len(owned)
            + [pl.BlockSpec(block, lambda r, me, flip: (r, 0, 0, 0))],
            out_specs=pl.BlockSpec((1, width_pno, width_pno), lambda r, me, flip: (r, 0, 0)),
        ),
        compiler_params=params(),
        cost_estimate=cost(2 * other.size * width_pno, 4 * other.size),
        name="couple_here",
    )(me, flip, *owned, other)


def weigh_here_kernel(capacity, parts, me_ref, *refs):
    partial = refs[:parts]
    facts_ref, rows_ref, out_ref = refs[parts:]
    facts = facts_ref[0].astype(F32)
    levels = join3(facts[1:2], facts[2:3], facts[3:4])
    fsum = join3(facts[4:5], facts[5:6], facts[6:7])
    count = facts[0:1, capacity : capacity + 1].astype(I32)
    amplitude = amplitudes(total(partial), levels, fsum, count)
    weights = (2.0 * amplitude - amplitude.T).astype(BF16)
    spread(
        out_ref.at[0],
        jnp.dot(weights, wide(rows_ref.at[0]), preferred_element_type=F32).astype(BF16),
    )


def weigh_here(me, partial, coef, rows, width_dom, capacity):
    groups, columns, width_pno, _ = rows.shape
    square = pl.BlockSpec((1, width_pno, width_pno), lambda r, me: (r, 0, 0))
    block = pl.BlockSpec((1, columns, width_pno, width_pno), lambda r, me: (r, 0, 0, 0))
    facts = pl.BlockSpec(
        (1, EXTRA, width_pno),
        lambda r, me: (partner(me[0], r, groups), width_dom // EXTRA, 0),
    )
    return pl.pallas_call(
        functools.partial(weigh_here_kernel, capacity, len(partial)),
        out_shape=jax.ShapeDtypeStruct(rows.shape, BF16),
        grid_spec=pltpu.PrefetchScalarGridSpec(
            num_scalar_prefetch=1,
            grid=(groups,),
            in_specs=[square] * len(partial) + [facts, block],
            out_specs=block,
        ),
        compiler_params=params(),
        cost_estimate=cost(2 * rows.size * width_pno, 4 * rows.size),
        name="weigh_here",
    )(me, *partial, coef, rows)


def gather_kernel(groups, places, me_ref, flip_ref, order_ref, start_ref, rows_ref, gamma_ref, *refs):
    coefs, (out_ref, gbuf, gsem, cbuf, csem) = refs[:places], refs[places:]
    o = pl.program_id(0)
    couples = start_ref[pl.num_programs(0)] // 2
    depth = gbuf.shape[0]
    width_dom = cbuf.shape[2]

    def fetch(u):
        at = lax.rem(u, depth)
        for n in range(2):
            slot = order_ref[2 * u + n]

            @pl.when(slot >= 0)
            def _():
                place, owner = split_slot(groups, slot)
                rank = place ^ flip_ref[0]
                lane = partner(me_ref[0], owner, groups)
                home = rank * groups + jnp.where(rank == 0, lane, owner)
                fetch_slot(groups, 0, home, [rows_ref], gamma_ref, gbuf.at[at, n], gsem.at[at, n])

                for c, ref in enumerate(coefs):

                    @pl.when(place == c)
                    def _():
                        pltpu.make_async_copy(
                            ref.at[owner, pl.ds(0, width_dom)], cbuf.at[at, n], csem.at[at, n]
                        ).start()

    @pl.when(o == 0)
    def _():
        for u in range(depth - 1):

            @pl.when(u < couples)
            def _():
                fetch(u)

    out_ref[...] = jnp.zeros_like(out_ref)

    @pl.loop(start_ref[o] // 2, start_ref[o + 1] // 2)
    def _(u):
        @pl.when(u + depth - 1 < couples)
        def _():
            fetch(u + depth - 1)

        at = lax.rem(u, depth)
        for n in range(2):
            slot = order_ref[2 * u + n]

            @pl.when(slot >= 0)
            def _():
                wait_slot(gamma_ref, gbuf.at[at, n], gsem.at[at, n])
                pltpu.make_async_copy(
                    coefs[0].at[0, pl.ds(0, width_dom)], cbuf.at[at, n], csem.at[at, n]
                ).wait()

        second = order_ref[2 * u + 1]

        @pl.when(second >= 0)
        def _():
            left = jnp.concatenate([cbuf[at, 0], cbuf[at, 1]], axis=1)
            right = jnp.concatenate([wide(gbuf.at[at, 0]), wide(gbuf.at[at, 1])], axis=0)
            out_ref[0] += jnp.dot(left, right, preferred_element_type=F32)

        @pl.when(second < 0)
        def _():
            out_ref[0] += jnp.dot(cbuf[at, 0], wide(gbuf.at[at, 0]), preferred_element_type=F32)


def gather_terms(me, flip, order, start, rows, gamma, coefs, occ_dev, width_dom):
    groups, columns, width_pno, _ = rows.shape
    width_aux = columns * width_pno
    places = len(coefs)
    depth = 5
    slots = groups * places
    return pl.pallas_call(
        functools.partial(gather_kernel, groups, places),
        out_shape=jax.ShapeDtypeStruct((occ_dev, width_dom, width_aux), F32),
        grid_spec=pltpu.PrefetchScalarGridSpec(
            num_scalar_prefetch=4,
            grid=(occ_dev,),
            in_specs=[ANY] * (2 + places),
            out_specs=pl.BlockSpec((1, width_dom, width_aux), lambda o, *_: (o, 0, 0)),
            scratch_shapes=[
                pltpu.VMEM((depth, 2, columns, width_pno, width_pno), BF16),
                pltpu.SemaphoreType.DMA((depth, 2)),
                pltpu.VMEM((depth, 2, width_dom, width_pno), BF16),
                pltpu.SemaphoreType.DMA((depth, 2)),
            ],
        ),
        compiler_params=params(),
        cost_estimate=cost(
            2 * slots * width_dom * width_pno * width_aux,
            2 * slots * width_pno * width_aux + 4 * occ_dev * width_dom * width_aux,
        ),
        name="gather_terms",
    )(me, flip, order, start, rows, gamma, *coefs)


def exchange(x):
    return lax.all_to_all(x, "pair", split_axis=0, concat_axis=0, tiled=True)


def crossed(lanes):
    groups = len(lanes)
    lanes = list(lanes)
    for r in reversed(range(1, groups)):
        lanes[r] = lax.ppermute(lanes[r], "pair", [(i, i ^ r) for i in range(groups)])
    return lanes


def swap(x):
    return lax.ppermute(x, "aux", [(0, 1), (1, 0)])


def body(three_index, fock_diag, pair_occ, pno_count, pno_energy, pno_coef):
    groups = lax.axis_size("pair")
    twins = lax.axis_size("aux") == 2
    occ_dev, width_dom, _ = three_index.shape
    pairs = pair_occ.shape[0]
    width_pno = pno_coef.shape[3]
    halves = 2 * pairs
    capacity = max(2, halves // groups + 1)
    capacity += capacity % 2
    flip = (lax.axis_index("aux") if twins else jnp.int32(0)).astype(I32).reshape(1)
    slot_of, home, inv, lead, request, fsum = index_tables(
        flip, pair_occ, fock_diag, occ_dev, groups, capacity
    )
    coef_half = pno_coef.reshape(halves, width_dom, width_pno)
    tables = (inv, lead, request, fsum, pno_count, pno_energy)
    coefs = []
    for place in range(capacity):
        if twins and place % 2:
            coefs.append(swap(coefs[-1]))
        else:
            packed = pack(tables, coef_half, place, groups, capacity)
            coefs.append(exchange(packed))
    arrived = coefs[0][:, width_dom, :capacity].astype(F32).astype(I32)
    columns = three_index.shape[2] // width_pno
    me = lax.axis_index("pair").astype(I32).reshape(1)
    if groups & (groups - 1):
        own = project(arrived, coefs, three_index, (0,))
        first = [exchange(own)]
    else:
        own, first = project_lanes(me, arrived, coefs[0], three_index)
        first = crossed(first)
    own_rest = project(arrived, coefs, three_index, tuple(range(1, capacity)))
    rest = exchange(own_rest)
    relayed = relay(me, lead, slot_of, first, rest, columns)
    if groups & (groups - 1):
        relayed = exchange(jnp.stack(relayed))
    else:
        relayed = crossed(relayed)
    rounded = BF16 if twins else F32

    def complete(mine):
        return [mine, swap(mine)] if twins else [lax.psum(mine, "aux")]

    mine = couple(me, slot_of, first, rest, pairs, columns, rounded)
    partial = complete(mine)
    gamma, energy = weigh(
        me, slot_of, home, pno_count, fsum, partial, pno_energy, first, rest, columns
    )
    gamma = exchange(gamma)
    order, start = order_tables(arrived, occ_dev)
    if isinstance(relayed, list):
        relayed = jnp.stack(relayed)
    partial = complete(couple_here(me, flip, [own, own_rest] if twins else [own], relayed, rounded))
    relayed = weigh_here(me, partial, coefs[0], relayed, width_dom, capacity)
    grad = gather_terms(me, flip, order, start, relayed, gamma, coefs, occ_dev, width_dom)
    return jnp.sum(energy, axis=1) / (width_pno * width_pno), grad


def solution(mesh):
    placed = (
        P("pair", None, "aux"),
        P(),
        P("pair", None),
        P("pair"),
        P("pair", None),
        P("pair", None, None, None),
    )
    return jax.shard_map(
        body,
        mesh=mesh,
        in_specs=placed,
        out_specs=(P("pair"), P("pair", None, "aux")),
        check_vma=False,
    )
```
